32 devices in a mesh: row: 8 (over z, x), col: 4 (over y, core).
Axes of the slice: x: 2, y: 2, z: 4, core: 2. Of those that a mesh axis runs over, the one named last changes fastest.
Arguments:
- panel_block: float32 [24576, 512], P('row', 'col'), may hold values from -1 to 1
- trailing: float32 [24576, 2048], P('row', 'col'), may hold values from -6 to 6
Outputs:
- triangle: float32 [512, 512], replicated
- coupling: float32 [512, 2048], P(None, 'col')
- updated: float32 [24576, 2048], P('row', 'col')
The draws below stay inside these ranges and needn't reach their ends.
All inputs are finite; a program needn't handle non-finite values.
Results may differ from the reference program's by a relative error of at most 0.0003.
Values sent between devices are 32-bit elements; how exact they have to be, the bound alone decides.
A program may use at most 128 MiB of HBM per device.

```python
import jax
import jax.numpy as jnp
from jax import lax

B = 512
NC = 2048
ROWS = 24576


def draw_panel_block(key, part):
    first_key, second_key = jax.random.split(key)
    base = jax.random.normal(first_key, (ROWS, B), jnp.float32)
    mixing = jnp.eye(B, dtype=jnp.float32) + 0.6 * jax.random.normal(second_key, (B, B), jnp.float32) / B ** 0.5
    return jnp.dot(base, mixing, precision=lax.Precision.HIGHEST) * ROWS ** (-0.5)


def block_scale(rng, dims, pieces, low, top_value):
    gain = 1.0
    for position, shards_of in pieces:
        steps = jax.random.uniform(jax.random.fold_in(jax.random.fold_in(rng, 6), position), (shards_of,), jnp.float32, low / len(pieces), top_value / len(pieces))
        gain = gain * jnp.repeat(jnp.exp(steps), dims[position] // shards_of).reshape((-1,) + (1,) * (len(dims) - 1 - position))
    return gain


def bell_draw(own_key, dims, scale, reach, cuts=(), kind=jnp.bfloat16):
    factor_of = block_scale(own_key, dims, cuts, -0.22, 0.18) if cuts else 1.0
    result = jax.random.normal(own_key, dims, jnp.float32) * scale * factor_of
    return jnp.minimum(jnp.maximum(result, -reach), reach).astype(kind)


def setup_inputs(seed: int = 0) -> dict:
    seeds = jax.random.split(jax.random.key(seed), 3)
    return {
        "panel_block": draw_panel_block(jax.random.fold_in(seeds[2], 71), 0),
        "trailing": bell_draw(seeds[1], (ROWS, NC), 1.0, 6.0, ((0, 8), (1, 4)), jnp.float32),
    }


def reference(panel_block, trailing):
    orthonormal, triangle = jnp.linalg.qr(panel_block)
    sign_fix = jnp.where(jnp.diagonal(triangle) < 0, -1.0, 1.0).astype(jnp.float32)
    triangle = triangle * sign_fix[:, None]
    orthonormal = orthonormal * sign_fix[None, :]
    coupling = jnp.dot(orthonormal.T.astype(jnp.float32), trailing.astype(jnp.float32), precision=lax.Precision.HIGHEST, preferred_element_type=jnp.float32)
    updated = trailing - jnp.dot(orthonormal.astype(jnp.float32), coupling.astype(jnp.float32), precision=lax.Precision.HIGHEST, preferred_element_type=jnp.float32)
    return (triangle, coupling, updated)
```

```python
import functools

import jax
import jax.numpy as jnp
from jax import lax
from jax.experimental import pallas as pl
from jax.experimental.pallas import tpu as pltpu
from jax.sharding import PartitionSpec as P

LANES = 128
SUB = 8
highest = lax.Precision.HIGHEST
high = lax.Precision.HIGH


def inner_products(left, right, precision=high):
    return lax.dot_general(
        left, right, (((0,), (0,)), ((), ())), precision=precision, preferred_element_type=jnp.float32
    )


def matmul(left, right, precision=high):
    return jnp.dot(left, right, precision=precision, preferred_element_type=jnp.float32)


def split3(x):
    top = x.astype(jnp.bfloat16).astype(jnp.float32)
    rest = x - top
    mid = rest.astype(jnp.bfloat16).astype(jnp.float32)
    return top, mid, rest - mid


def rank_update(left, right):
    lt, lm, ll = split3(left)
    rt, rm, rl = split3(right)
    a = jnp.concatenate([lt, lt, lm, lt, ll, lm], axis=0).astype(jnp.bfloat16)
    b = jnp.concatenate([rt, rm, rt, rl, rt, rm], axis=0).astype(jnp.bfloat16)
    return lax.dot_general(a, b, (((0,), (0,)), ((), ())), preferred_element_type=jnp.float32)


def factor_diagonal(square, hook=None):
    lane = lax.broadcasted_iota(jnp.int32, (SUB, LANES), 1)
    sub = lax.broadcasted_iota(jnp.int32, (SUB, LANES), 0)
    full = (SUB, LANES)
    work = square
    upper_rows, inverse_rows = [], []
    for first in range(0, LANES, SUB):
        if hook is not None:
            hook(first // SUB)
        rows = work[:SUB]
        b = [jnp.broadcast_to(rows[t : t + 1, :], full) for t in range(SUB)]
        d = [
            [None if s < t else jnp.broadcast_to(b[t][:, first + s : first + s + 1], full) for s in range(SUB)]
            for t in range(SUB)
        ]
        inside = (lane >= first) & (lane < first + SUB)
        unit = [jnp.where(inside, jnp.where(lane == first + t, 1.0, 0.0), b[t]) for t in range(SUB)]
        tri = jnp.zeros(full, jnp.float32)
        out = jnp.zeros(full, jnp.float32)
        for t in range(SUB):
            inv = 1.0 / jnp.sqrt(d[t][t])
            for s in range(t, SUB):
                d[t][s] = d[t][s] * inv
            x = unit[t] * inv
            for s in range(t + 1, SUB):
                for q in range(s, SUB):
                    d[s][q] = d[s][q] - d[t][s] * d[t][q]
                unit[s] = unit[s] - d[t][s] * x
            line = x
            for s in range(SUB):
                line = jnp.where(lane == first + s, d[t][s] if s >= t else 0.0, line)
            tri = jnp.where(sub == t, line, tri)
            out = jnp.where(sub == t, x, out)
        upper_rows.append(jnp.where(lane >= first, tri, 0.0))
        inverse_rows.append(jnp.where(lane < first + SUB, out, 0.0))
        if first + SUB < LANES:
            beyond = jnp.where(lane >= first + SUB, out, 0.0)
            left = work[SUB:]
            place = lax.broadcasted_iota(jnp.int32, left.shape, 1)
            left = jnp.where((place >= first) & (place < first + SUB), 0.0, left)
            work = left - rank_update(beyond, out)[first + SUB :]
    return jnp.concatenate(upper_rows, axis=0), jnp.concatenate(inverse_rows, axis=0)


def factor_kernel(gram_ref, upper_ref, inverse_ref, work):
    width = gram_ref.shape[0]
    work[...] = gram_ref[...]
    upper_ref[...] = jnp.zeros_like(upper_ref)
    inverse_ref[...] = jnp.zeros_like(inverse_ref)
    lanes_all = lax.broadcasted_iota(jnp.int32, (LANES, width), 1)

    @pl.loop(0, width // LANES)
    def _(k):
        at = pl.multiple_of(k * LANES, LANES)
        here = pl.ds(at, LANES)
        upper, inverse = factor_diagonal(work[here, here])
        rows = matmul(inverse, work[here, :], highest)
        upper_ref[here, :] = jnp.where(lanes_all >= at + LANES, rows, 0.0)
        upper_ref[here, here] = upper
        inverse_ref[here, :] = jnp.where(lanes_all < at, rows, 0.0)
        inverse_ref[here, here] = inverse
        work[here, :] = rows
        work[here, here] = inverse
        done = work[here, :]
        right = upper_ref[here, :]
        for i in range(1, width // LANES):
            @pl.when(i > k)
            def _():
                block = slice(i * LANES, (i + 1) * LANES)
                below = inner_products(right[:, block], done, highest)
                old = jnp.where((lanes_all >= at) & (lanes_all < at + LANES), 0.0, work[block, :])
                work[block, :] = old - below


def factor(gram):
    width = gram.shape[0]
    spec = pl.BlockSpec(memory_space=pltpu.VMEM)
    shape = jax.ShapeDtypeStruct((width, width), jnp.float32)
    return pl.pallas_call(
        factor_kernel,
        out_shape=(shape, shape),
        in_specs=[spec],
        out_specs=(spec, spec),
        scratch_shapes=[pltpu.VMEM((width, width), jnp.float32)],
        cost_estimate=pl.CostEstimate(
            flops=4 * width**3, bytes_accessed=12 * width * width, transcendentals=100000
        ),
        name="factor",
    )(gram)


def gram_kernel(nr, nc, part_ref, out_ref, heard, total, blocks, send, recv, give, take, pass_on, get):
    my_row = lax.axis_index("row")
    my_col = lax.axis_index("col")
    size = part_ref.shape[0] // nr
    wide = part_ref.shape[1]
    mesh_id = pl.DeviceIdType.MESH

    def rows_of(row):
        return pl.ds(pl.multiple_of(row * size, size), size)

    def row_peer(k):
        return lax.rem(my_row + k, nr)

    def col_peer(j):
        return lax.rem(my_col + j, nc)

    barrier = pltpu.get_barrier_semaphore()
    for k in range(1, nr):
        pl.semaphore_signal(barrier, inc=1, device_id=(row_peer(k), my_col), device_id_type=mesh_id)
    for j in range(1, nc):
        pl.semaphore_signal(barrier, inc=1, device_id=(my_row, col_peer(j)), device_id_type=mesh_id)
    pl.semaphore_wait(barrier, nr + nc - 2)

    first = [
        pltpu.make_async_remote_copy(
            src_ref=part_ref.at[rows_of(row_peer(k))],
            dst_ref=heard.at[k],
            send_sem=send.at[k],
            recv_sem=recv.at[k],
            device_id=(row_peer(k), my_col),
            device_id_type=mesh_id,
        )
        for k in range(1, nr)
    ]
    for copy in first:
        copy.start()
    value = part_ref[rows_of(my_row), :]
    for k, copy in enumerate(first, 1):
        copy.wait_recv()
        value = value + heard[k]
    total[...] = value

    def spread(k, j, block):
        return pltpu.make_async_remote_copy(
            src_ref=block,
            dst_ref=blocks.at[my_col, rows_of(lax.rem(my_row - k + nr, nr))],
            send_sem=pass_on.at[k, j],
            recv_sem=get.at[k, j],
            device_id=(my_row, col_peer(j)),
            device_id_type=mesh_id,
        )

    second = [
        pltpu.make_async_remote_copy(
            src_ref=total,
            dst_ref=blocks.at[my_col, rows_of(my_row)],
            send_sem=give.at[k],
            recv_sem=take.at[k],
            device_id=(row_peer(k), my_col),
            device_id_type=mesh_id,
        )
        for k in range(1, nr)
    ]
    for copy in second:
        copy.start()
    third = [spread(0, j, total) for j in range(1, nc)]
    for copy in third:
        copy.start()
    blocks[my_col, rows_of(my_row), :] = value
    for k, copy in enumerate(second, 1):
        copy.wait_recv()
        block = blocks.at[my_col, rows_of(lax.rem(my_row - k + nr, nr))]
        for j in range(1, nc):
            hop = spread(k, j, block)
            hop.start()
            third.append(hop)
    for copy in third:
        copy.wait_recv()
    for c in range(nc):
        out_ref[:, c * wide : (c + 1) * wide] = blocks[c]
    for copy in first + second + third:
        copy.wait_send()


def sum_gram(part, nr, nc):
    width, wide = part.shape
    spec = pl.BlockSpec(memory_space=pltpu.VMEM)
    dma = pltpu.SemaphoreType.DMA
    return pl.pallas_call(
        functools.partial(gram_kernel, nr, nc),
        out_shape=jax.ShapeDtypeStruct((width, wide * nc), jnp.float32),
        in_specs=[spec],
        out_specs=spec,
        scratch_shapes=[
            pltpu.VMEM((nr, width // nr, wide), jnp.float32),
            pltpu.VMEM((width // nr, wide), jnp.float32),
            pltpu.VMEM((nc, width, wide), jnp.float32),
            dma((nr,)),
            dma((nr,)),
            dma((nr,)),
            dma((nr,)),
            dma((nr, nc)),
            dma((nr, nc)),
        ],
        compiler_params=pltpu.CompilerParams(collective_id=0, has_side_effects=True),
        cost_estimate=pl.CostEstimate(
            flops=100000, bytes_accessed=20000000, transcendentals=0
        ),
        name="sum_gram",
    )(part)


def split2(x):
    top = x.astype(jnp.bfloat16)
    return top, (x - top.astype(jnp.float32)).astype(jnp.bfloat16)


def dot3(left, right, dims=(((1,), (0,)), ((), ()))):
    def one(a, b):
        return lax.dot_general(a, b, dims, preferred_element_type=jnp.float32)

    return one(left[0], right[0]) + (one(left[0], right[1]) + one(left[1], right[0]))


def update_kernel(panel_ref, weights_ref, trailing_ref, out_ref, top, low):
    @pl.when(pl.program_id(0) == 0)
    def _():
        top[...], low[...] = split2(weights_ref[...])

    pt, pm = split2(panel_ref[...])

    def product(left, right):
        return jnp.dot(left, right[...], preferred_element_type=jnp.float32)

    out_ref[...] = trailing_ref[...] - (product(pt, top) + (product(pt, low) + product(pm, top)))


def update(panel, weights, trailing):
    rows, width = panel.shape
    columns = trailing.shape[1]
    tile = next((t for t in (384, 256, 128, 64, 8) if rows % t == 0), rows)
    return pl.pallas_call(
        update_kernel,
        grid=(rows // tile,),
        out_shape=jax.ShapeDtypeStruct(trailing.shape, jnp.float32),
        in_specs=[
            pl.BlockSpec((tile, width), lambda i: (i, 0)),
            pl.BlockSpec((width, columns), lambda i: (0, 0)),
            pl.BlockSpec((tile, columns), lambda i: (i, 0)),
        ],
        out_specs=pl.BlockSpec((tile, columns), lambda i: (i, 0)),
        scratch_shapes=[pltpu.VMEM((width, columns), jnp.bfloat16)] * 2,
        cost_estimate=pl.CostEstimate(
            flops=6 * rows * width * columns,
            bytes_accessed=4 * (rows * width + 2 * rows * columns),
            transcendentals=0,
        ),
        name="update",
    )(panel, weights, trailing)


def gather_kernel(nc, pieces, block_ref, out_ref, send, recv, pass_on, get, near):
    my_row = lax.axis_index("row")
    my_col = lax.axis_index("col")
    rows, wide = block_ref.shape
    size = rows // pieces
    mesh_id = pl.DeviceIdType.MESH
    core = lax.rem(my_col, 2)
    partner = my_col + 1 - 2 * core

    def across(j):
        return lax.rem(my_col + 2 * j, nc)

    def columns(col):
        return pl.ds(pl.multiple_of(col * wide, wide), wide)

    def remote(src, dst, send_sem, recv_sem, col):
        return pltpu.make_async_remote_copy(
            src_ref=src, dst_ref=dst, send_sem=send_sem, recv_sem=recv_sem,
            device_id=(my_row, col), device_id_type=mesh_id,
        )

    barrier = pltpu.get_barrier_semaphore()
    pl.semaphore_signal(barrier, inc=1, device_id=(my_row, partner), device_id_type=mesh_id)
    for j in range(1, nc // 2):
        pl.semaphore_signal(barrier, inc=1, device_id=(my_row, across(j)), device_id_type=mesh_id)
    pl.semaphore_wait(barrier, nc // 2)

    far = []
    for p in range(pieces):
        here = pl.ds(p * size, size)
        for j in range(1, nc // 2):
            copy = remote(
                block_ref.at[here], out_ref.at[here, columns(my_col)],
                send.at[j, p], recv.at[j, p], across(j),
            )
            copy.start()
            far.append((p, j, copy))
    beside = remote(block_ref, out_ref.at[:, columns(my_col)], near.at[0], near.at[1], partner)
    beside.start()
    own = pltpu.make_async_copy(block_ref, out_ref.at[:, columns(my_col)], near.at[2])
    own.start()
    for p, j, copy in far:
        copy.wait_recv()
        source = lax.rem(my_col - 2 * j + nc, nc)
        spot = out_ref.at[pl.ds(p * size, size), columns(source)]
        hop = remote(spot, spot, pass_on.at[j, p], get.at[j, p], partner)
        hop.start()
        hops.append(hop)
    own.wait()
    beside.wait()
    for hop in hops:
        hop.wait()
    for _, _, copy in far:
        copy.wait_send()


def gather_panel(block, nc):
    rows, wide = block.shape
    pieces = 8
    if nc % 2 or wide % LANES or rows % (SUB * pieces):
        return lax.all_gather(block, "col", axis=1, tiled=True)
    dma = pltpu.SemaphoreType.DMA
    return pl.pallas_call(
        functools.partial(gather_kernel, nc, pieces),
        out_shape=jax.ShapeDtypeStruct((rows, wide * nc), jnp.float32),
        in_specs=[pl.BlockSpec(memory_space=pltpu.VMEM)],
        out_specs=pl.BlockSpec(memory_space=pl.ANY),
        scratch_shapes=[dma((nc // 2, pieces))] * 4 + [dma((3,))],
        compiler_params=pltpu.CompilerParams(collective_id=1, has_side_effects=True),
        name="gather_panel",
    )(block)


def general(nr, nc, panel_block, trailing):
    gathered = gather_panel(panel_block, nc)
    share = inner_products(gathered, trailing)
    projected = lax.psum(share, "row")
    gathered, share = lax.optimization_barrier((gathered, share))
    gram = sum_gram(inner_products(gathered, panel_block), nr, nc)
    upper, inverse = factor(gram)
    coupling = matmul(inverse, projected)
    weights = inner_products(inverse, coupling)
    updated = update(gathered, weights, trailing)
    return (upper, coupling, updated)


class Place:
    def __init__(self, nr):
        self.nr, self.nx = nr, 2
        self.nz = nr // 2
        self.row, self.col = lax.axis_index("row"), lax.axis_index("col")
        self.z, self.x = self.row // 2, lax.rem(self.row, 2)
        self.y, self.core = self.col // 2, lax.rem(self.col, 2)
        self.partner = (self.row, self.y * 2 + 1 - self.core)
        self.across = (self.row, (1 - self.y) * 2 + self.core)
        self.beside = (self.z * 2 + 1 - self.x, self.col)

    def level(self, j):
        return lax.rem(self.z + j, self.nz)

    def along(self, j):
        return (self.level(j) * 2 + self.x, self.col)

    def far(self, dy, dr):
        y = self.y + dy - 2 * dy * self.y
        return (lax.rem(self.row + dr, self.nr), y * 2 + self.core)


def remote(src, dst, send, recv, device):
    return pltpu.make_async_remote_copy(
        src_ref=src, dst_ref=dst, send_sem=send, recv_sem=recv,
        device_id=device, device_id_type=pl.DeviceIdType.MESH,
    )


def part(start, size, multiple=None):
    if isinstance(start, int):
        return pl.ds(start, size)
    return pl.ds(pl.multiple_of(start, multiple or size), size)


class RowSum:
    def __init__(self, at, share, from_x, from_z, out, sems):
        self.at, self.share, self.from_x, self.from_z, self.out = at, share, from_x, from_z, out
        self.send, self.recv = sems.at[0], sems.at[1]
        self.half = share.shape[0] // 2
        self.slice = self.half // at.nz
        self.sent = []

    def go(self, stage, j, ends):
        def make():
            src, dst, device = ends()
            return remote(src, dst, self.send.at[stage, j], self.recv.at[stage, j], device)

        make().start()
        self.sent.append(make)

    def landed(self, stage, j, dst):
        remote(dst, dst, self.send.at[stage, j], self.recv.at[stage, j], self.at.beside).wait_recv()

    def rows(self, x, z):
        return part(x * self.half + z * self.slice, self.slice)

    def over_x(self):
        self.go(0, 0, lambda: (
            self.share.at[part((1 - self.at.x) * self.half, self.half)], self.from_x, self.at.beside
        ))

    def over_z(self):
        self.landed(0, 0, self.from_x)
        mine = part(self.at.x * self.half, self.half)
        self.share[mine, :] = self.share[mine, :] + self.from_x[...]
        for j in range(1, self.at.nz):
            self.go(1, j, lambda j=j: (
                self.share.at[self.rows(self.at.x, self.at.level(j))], self.from_z.at[j], self.at.along(j)
            ))

    def give(self):
        here = self.rows(self.at.x, self.at.z)
        value = self.share[here, :]
        for j in range(1, self.at.nz):
            self.landed(1, j, self.from_z.at[j])
            value = value + self.from_z[j]
        self.out[here, :] = value

        def spot():
            return self.out.at[self.rows(self.at.x, self.at.z)]

        for j in range(1, self.at.nz):
            self.go(2, j, lambda j=j: (spot(), spot(), self.at.along(j)))
        self.go(3, 0, lambda: (spot(), spot(), self.at.beside))

    def back_x(self):
        for j in range(1, self.at.nz):
            def spot(j=j):
                return self.out.at[self.rows(self.at.x, self.at.level(self.at.nz - j))]

            self.landed(2, j, spot())
            self.go(3, j, lambda spot=spot: (spot(), spot(), self.at.beside))

    def finish(self):
        for j in range(self.at.nz):
            self.landed(3, j, self.out.at[self.rows(1 - self.at.x, self.at.level((self.at.nz - j) % self.at.nz))])

    def close(self):
        for make in self.sent:
            make().wait_send()


def panel_kernel(
    nr, pieces, chunk, block_ref, trailing_ref, panel_ref, upper_ref, inverse_ref, summed_ref,
    blk, tbuf, tth, ttl, gpart, cpart, heard_o, heard_c, own_g, cross_g,
    share_o, share_r, from_x_o, from_z_o, out_o, from_x_r, from_z_r, out_r,
    dia, du, di, half_g, half_u, half_i, row_r, cross_x,
    near, ysend, yrecv, fsend, frecv, o_sems, oa_sems, c_sems, ca_sems, g_sems, sum_sems, local,
):
    at = Place(nr)
    rows, wide = block_ref.shape
    half = rows // 2
    y, core, col = at.y, at.core, at.col
    pair = 2 * y
    away = 2 * (1 - y)
    size = half // pieces
    quarter = half // 4

    fetch = pltpu.make_async_copy(trailing_ref, tbuf, local.at[0])
    fetch.start()
    keep = pltpu.make_async_copy(block_ref, blk.at[col], local.at[1])
    keep.start()

    peers = [(dy, dr) for dy in range(2) for dr in range(nr) if dy or dr]
    barrier = pltpu.get_barrier_semaphore()
    for dy, dr in peers:
        pl.semaphore_signal(barrier, inc=1, device_id=at.far(dy, dr), device_id_type=pl.DeviceIdType.MESH)
    pl.semaphore_signal(barrier, inc=1, device_id=at.partner, device_id_type=pl.DeviceIdType.MESH)
    pl.semaphore_wait(barrier, len(peers) + 1)

    beside = remote(block_ref, blk.at[col], near.at[0], near.at[1], at.partner)
    first = [
        remote(
            block_ref.at[part((1 - y) * half + p * size, size)],
            blk.at[col, part((1 - y) * half + p * size, size)],
            ysend.at[p], yrecv.at[p], at.across,
        )
        for p in range(pieces)
    ]
    second = []
    for b in range(2):
        for p in range(2):
            i = pieces + 2 * b + p
            spot = blk.at[pair + b, part(y * half + core * 2 * quarter + p * quarter, quarter)]
            second.append(remote(spot, spot, ysend.at[i], yrecv.at[i], at.across))
    queue = first + second

    def follow(i):
        if i + 2 < len(queue):
            queue[i].wait_send()
            queue[i + 2].start()

    def arrived(i):
        if i < pieces:
            block, where = away + core, part(y * half + i * size, size)
        else:
            b, p = divmod(i - pieces, 2)
            block, where = away + b, part((1 - y) * half + core * 2 * quarter + p * quarter, quarter)
        spot = blk.at[block, where]
        remote(spot, spot, ysend.at[i], yrecv.at[i], at.across).wait_recv()
        remote(spot, spot, fsend.at[i], frecv.at[i], at.partner).start()

    def handed(i):
        if i < pieces:
            block, where = away + 1 - core, part(y * half + i * size, size)
        else:
            b, p = divmod(i - pieces, 2)
            block, where = away + b, part((1 - y) * half + (1 - core) * 2 * quarter + p * quarter, quarter)
        spot = blk.at[block, where]
        remote(spot, spot, fsend.at[i], frecv.at[i], at.partner).wait_recv()

    beside.start()
    queue[0].start()
    queue[1].start()
    keep.wait()

    beside.wait_recv()
    gpart[...] = jnp.zeros_like(gpart)

    @pl.loop(0, rows // chunk)
    def _(i):
        here = part(i * chunk, chunk)
        turned = split2(blk[col, here, :].T)
        right = split2(jnp.concatenate([blk[pair, here, :], blk[pair + 1, here, :]], axis=1))
        gpart[...] += dot3(turned, right)

    gslice = wide // nr
    sent = [beside]
    made = []

    def go(ends):
        remote(*ends()).start()
        made.append(lambda: remote(*ends()))

    scatter = []
    for dr in range(1, nr):
        copy = remote(
            gpart.at[part(at.far(0, dr)[0] * gslice, gslice)], heard_o.at[dr],
            o_sems.at[0, dr], o_sems.at[1, dr], at.far(0, dr),
        )
        copy.start()
        scatter.append(copy)
        sent.append(copy)

    fetch.wait()
    share_o[...] = jnp.zeros_like(share_o)

    @pl.loop(0, rows // chunk)
    def _(i):
        here = part(i * chunk, chunk)
        high_part, low_part = split2(tbuf[here, :].T)
        tth[:, here], ttl[:, here] = high_part, low_part
        right = split2(jnp.concatenate([blk[pair, here, :], blk[pair + 1, here, :]], axis=1))
        share_o[...] += dot3((high_part, low_part), right)

    sums = [RowSum(at, share_o, from_x_o, from_z_o, out_o, sum_sems.at[0])]
    for b in range(2):
        sums.append(RowSum(at, share_r.at[b], from_x_r.at[b], from_z_r.at[b], out_r.at[b], sum_sems.at[1 + b]))

    def own_gram_sum():
        value = gpart[part(at.row * gslice, gslice), :]
        for dr, copy in enumerate(scatter, 1):
            copy.wait_recv()
            value = value + heard_o[dr]

        def spot():
            return own_g.at[col, part(at.row * gslice, gslice)]

        spot()[...] = value
        for dy, dr in peers:
            go(lambda dy=dy, dr=dr: (spot(), spot(), oa_sems.at[0, dy, dr], oa_sems.at[1, dy, dr], at.far(dy, dr)))

    def own_gram_forward():
        for dy in range(2):
            block = at.far(dy, 0)[1]
            whose = own_g.at[block]
            for dr in range(nr):
                if dy or dr:
                    spot = own_g.at[block, part(at.far(0, (nr - dr) % nr)[0] * gslice, gslice)]
                    remote(spot, spot, oa_sems.at[0, dy, dr], oa_sems.at[1, dy, dr], at.partner).wait_recv()
            copy = remote(whose, whose, g_sems.at[0, dy], g_sems.at[1, dy], at.partner)
            copy.start()
            sent.append(copy)

    def own_gram_done(dy):
        spot = own_g.at[at.far(dy, 0)[1] + 1 - 2 * core]
        remote(spot, spot, g_sems.at[0, dy], g_sems.at[1, dy], at.partner).wait_recv()

    cslice = wide // (2 * nr)

    def cross_rows(dy, dr, back=False):
        row = lax.rem(at.row + ((nr - dr) % nr if back else dr), nr)
        other = y + dy - 2 * dy * y
        return part((other * nr + row) * cslice, cslice)

    def cross_scatter():
        for dy, dr in peers:
            copy = remote(
                cpart.at[cross_rows(dy, dr)], heard_c.at[dy, dr],
                c_sems.at[0, dy, dr], c_sems.at[1, dy, dr], at.far(dy, dr),
            )
            copy.start()
            sent.append(copy)

    def cross_sum():
        value = cpart[cross_rows(0, 0), :]
        for dy, dr in peers:
            spot = heard_c.at[dy, dr]
            remote(spot, spot, c_sems.at[0, dy, dr], c_sems.at[1, dy, dr], at.partner).wait_recv()
            value = value + heard_c[dy, dr]

        def spot():
            return cross_g.at[core, cross_rows(0, 0)]

        spot()[...] = value
        for dy, dr in peers:
            go(lambda dy=dy, dr=dr: (spot(), spot(), ca_sems.at[0, dy, dr], ca_sems.at[1, dy, dr], at.far(dy, dr)))

    def cross_forward():
        for dy, dr in peers:
            spot = cross_g.at[core, cross_rows(dy, dr, back=True)]
            remote(spot, spot, ca_sems.at[0, dy, dr], ca_sems.at[1, dy, dr], at.partner).wait_recv()
        go(lambda: (cross_g.at[core], cross_g.at[core], g_sems.at[0, 2], g_sems.at[1, 2], at.partner))

    def cross_done():
        spot = cross_g.at[1 - core]
        remote(spot, spot, g_sems.at[0, 2], g_sems.at[1, 2], at.partner).wait_recv()

    def first_products(p):
        here = part(y * half + p * size, size)
        right = split2(jnp.concatenate([blk[away, here, :], blk[away + 1, here, :]], axis=1))
        value = dot3((tth[:, here], ttl[:, here]), right)
        turned = split2(blk[core, here, :].T)
        right = split2(jnp.concatenate([blk[2, here, :], blk[3, here, :]], axis=1))
        cross = dot3(turned, right)
        if p:
            for b in range(2):
                share_r[b] += value[:, b * wide : (b + 1) * wide]
            cpart[...] += cross
        else:
            for b in range(2):
                share_r[b] = value[:, b * wide : (b + 1) * wide]
            cpart[...] = cross

    def second_products(b, p):
        for k in range(2):
            here = part((1 - y) * half + k * 2 * quarter + p * quarter, quarter)
            share_r[b] += dot3((tth[:, here], ttl[:, here]), split2(blk[away + b, here, :]))

    sums[0].over_x()
    own_gram_sum()
    for p in range(pieces):
        arrived(p)
        follow(p)
        if p == 1:
            sums[0].over_z()
        if p:
            handed(p - 1)
            first_products(p - 1)
    handed(pieces - 1)
    first_products(pieces - 1)
    cross_scatter()
    own_gram_forward()
    own_gram_done(0)
    own_gram_done(1)
    sums[0].give()

    def late(b, p):
        handed(pieces + 2 * b + p)
        second_products(b, p)

    def come(b, p):
        arrived(pieces + 2 * b + p)
        follow(pieces + 2 * b + p)

    events = {
        (0, 4): [cross_sum],
        (0, 10): [sums[0].back_x],
        (1, 0): [lambda: come(0, 0)],
        (1, 4): [lambda: late(0, 0), cross_forward],
        (1, 12): [lambda: come(0, 1)],
        (2, 2): [lambda: late(0, 1), sums[1].over_x],
        (2, 6): [lambda: come(1, 0)],
        (2, 8): [lambda: late(1, 0), sums[1].over_z],
        (2, 13): [sums[1].give],
        (3, 0): [lambda: come(1, 1)],
        (3, 2): [lambda: late(1, 1), sums[2].over_x, sums[1].back_x],
        (3, 7): [sums[2].over_z],
        (3, 12): [sums[2].give],
    }

    def whole(left, right):
        return jnp.dot(left, right, precision=highest, preferred_element_type=jnp.float32)

    lo, hi = slice(0, wide), slice(wide, 2 * wide)
    both = slice(0, 2 * wide)

    def load_half(h):
        half_g[lo, :] = own_g[2 * h]
        half_g[hi, :] = own_g[2 * h + 1]

    upper_ref[...] = jnp.zeros_like(upper_ref)
    inverse_ref[...] = jnp.zeros_like(inverse_ref)
    load_half(0)
    dia[...] = half_g[lo, lo]

    def even(h):
        half_u[lo, lo], half_i[lo, lo] = du[...], di[...]
        rest = whole(di[...], half_g[lo, hi])
        row_r[...] = rest
        half_u[lo, hi] = rest
        half_u[hi, lo] = jnp.zeros_like(rest)
        half_i[lo, hi] = jnp.zeros_like(rest)
        dia[...] = half_g[hi, hi] - inner_products(rest, rest, highest)

    def odd(h):
        half_u[hi, hi], half_i[hi, hi] = du[...], di[...]
        below = inner_products(row_r[...], half_i[lo, lo], highest)
        half_i[hi, lo] = -whole(di[...], below)
        place = slice(h * 2 * wide, (h + 1) * 2 * wide)
        upper_ref[place, place] = half_u[...]
        inverse_ref[place, place] = half_i[...]

    top, end = slice(0, 2 * wide), slice(2 * wide, 4 * wide)

    def after0():
        even(0)

    def after1():
        odd(0)
        cross_done()
        load_half(1)
        corner = jnp.concatenate([cross_g[0], cross_g[1]], axis=0)
        right = whole(half_i[...], corner)
        cross_x[...] = right
        upper_ref[top, end] = right
        half_g[...] = half_g[...] - inner_products(right, right, highest)
        dia[...] = half_g[lo, lo]

    def after2():
        even(1)

    def after3():
        odd(1)
        below = inner_products(cross_x[...], inverse_ref[top, top], highest)
        inverse_ref[end, top] = -whole(half_i[...], below)

    @pl.loop(0, 4)
    def _(k):
        def hook(step):
            for (when, where), steps in events.items():
                if where == step:
                    @pl.when(k == when)
                    def _():
                        for one in steps:
                            one()

        du[...], di[...] = factor_diagonal(dia[...], hook)
        for when, step in enumerate((after0, after1, after2, after3)):
            pl.when(k == when)(step)

    out = []
    for b in range(4):
        copy = pltpu.make_async_copy(blk.at[b], panel_ref.at[:, b * wide : (b + 1) * wide], local.at[2 + b])
        copy.start()
        out.append(copy)
    sums[2].back_x()
    for one in sums:
        one.finish()
    summed_ref[:, part(pair * wide, 2 * wide)] = out_o[...]
    for b in range(2):
        summed_ref[:, part((away + b) * wide, wide)] = out_r[b]
    for copy in sent + queue[-2:]:
        copy.wait_send()
    for make in made:
        make().wait_send()
    for i in range(len(queue)):
        spot = blk.at[0, pl.ds(0, size if i < pieces else quarter)]
        remote(spot, spot, fsend.at[i], frecv.at[i], at.partner).wait_send()
    for one in sums:
        one.close()
    for copy in out:
        copy.wait()


def panel_pieces(rows, wide, nr, nc):
    if nc != 4 or nr % 2 or nr < 4 or wide % LANES or wide % (2 * SUB * nr) or rows % 8:
        return 0
    half = rows // 2
    if half % (4 * LANES):
        return 0
    return next((p for p in (3, 2) if half % (p * LANES) == 0), 0)


def factor_panel(block, trailing, nr, pieces):
    rows, wide = block.shape
    columns = trailing.shape[1]
    chunk = rows // 2 // pieces
    hbm, vmem = pl.BlockSpec(memory_space=pl.ANY), pl.BlockSpec(memory_space=pltpu.VMEM)
    f32, dma = jnp.float32, pltpu.SemaphoreType.DMA

    def room(*shape, dtype=f32):
        return pltpu.VMEM(shape, dtype)

    width = 4 * wide
    nz = nr // 2
    square = jax.ShapeDtypeStruct((width, width), f32)
    return pl.pallas_call(
        functools.partial(panel_kernel, nr, pieces, chunk),
        out_shape=(
            jax.ShapeDtypeStruct((rows, width), f32), square, square,
            jax.ShapeDtypeStruct((columns, width), f32),
        ),
        in_specs=[hbm, hbm],
        out_specs=(hbm, vmem, vmem, vmem),
        scratch_shapes=[
            room(4, rows, wide), room(rows, columns),
            room(columns, rows, dtype=jnp.bfloat16), room(columns, rows, dtype=jnp.bfloat16),

            room(wide, 2 * wide), room(wide, 2 * wide),
            room(nr, wide // nr, 2 * wide), room(2, nr, wide // (2 * nr), 2 * wide),
            room(4, wide, 2 * wide), room(2, wide, 2 * wide),
            room(columns, 2 * wide), room(2, columns, wide),
            room(columns // 2, 2 * wide), room(nz, columns // nr, 2 * wide), room(columns, 2 * wide),
            room(2, columns // 2, wide), room(2, nz, columns // nr, wide), room(2, columns, wide),
            room(wide, wide), room(wide, wide), room(wide, wide),
            room(2 * wide, 2 * wide), room(2 * wide, 2 * wide), room(2 * wide, 2 * wide),
            room(wide, wide), room(2 * wide, 2 * wide),
            dma((2,)), dma((pieces + 4,)), dma((pieces + 4,)), dma((pieces + 4,)), dma((pieces + 4,)),
            dma((2, nr)), dma((2, 2, nr)), dma((2, 2, nr)), dma((2, 2, nr)), dma((2, 3)),
            dma((3, 2, 4, nz)), dma((6,)),
        ],
        compiler_params=pltpu.CompilerParams(
            collective_id=2, has_side_effects=True, vmem_limit_bytes=48 * 1024 * 1024
        ),
        name="factor_panel",
    )(block, trailing)


def finish_kernel(panel_ref, inverse_ref, summed_ref, upper_ref, trailing_ref, out_ref, coupling_ref, triangle_ref, top, low):
    @pl.when(pl.program_id(0) == 0)
    def _():
        inverse = split2(inverse_ref[...])
        coupling = dot3(inverse, split2(summed_ref[...]), (((1,), (1,)), ((), ())))
        coupling_ref[...] = coupling
        triangle_ref[...] = upper_ref[...]
        turned = split2(inverse_ref[...].T)
        top[...], low[...] = split2(dot3(turned, split2(coupling)))

    panel = split2(panel_ref[...])
    out_ref[...] = trailing_ref[...] - dot3(panel, (top[...], low[...]))


def finish(panel, inverse, summed, upper, trailing):
    rows, width = panel.shape
    columns = trailing.shape[1]
    tile = next((t for t in (384, 256, 128, 64, 16) if rows % t == 0), rows)
    still = lambda shape: pl.BlockSpec(shape, lambda i: (0, 0))
    f32 = jnp.float32
    return pl.pallas_call(
        finish_kernel,
        grid=(rows // tile,),
        out_shape=(
            jax.ShapeDtypeStruct(trailing.shape, f32), jax.ShapeDtypeStruct((width, columns), f32),
            jax.ShapeDtypeStruct((width, width), f32),
        ),
        in_specs=[
            pl.BlockSpec((tile, width), lambda i: (i, 0)),
            still((width, width)), still((columns, width)), still((width, width)),
            pl.BlockSpec((tile, columns), lambda i: (i, 0)),
        ],
        out_specs=(pl.BlockSpec((tile, columns), lambda i: (i, 0)), still((width, columns)), still((width, width))),
        scratch_shapes=[pltpu.VMEM((width, columns), jnp.bfloat16)] * 2,
        compiler_params=pltpu.CompilerParams(vmem_limit_bytes=40 * 1024 * 1024),
        name="finish",
    )(panel, inverse, summed, upper, trailing)


def on_device(nr, nc, panel_block, trailing):
    rows, wide = panel_block.shape
    pieces = panel_pieces(rows, wide, nr, nc)
    if not pieces or trailing.shape[1] % (SUB * nr):
        return general(nr, nc, panel_block, trailing)
    panel, upper, inverse, summed = factor_panel(panel_block, trailing, nr, pieces)
    updated, coupling, triangle = finish(panel, inverse, summed, upper, trailing)
    return (triangle, coupling, updated)


def solution(mesh):
    placed = (P("row", "col"), P("row", "col"))
    return jax.shard_map(
        functools.partial(on_device, mesh.shape["row"], mesh.shape["col"]),
        mesh=mesh,
        in_specs=placed,
        out_specs=(P(), P(None, "col"), P("row", "col")),
        check_vma=False,
    )
```

```python
import functools

import jax
import jax.numpy as jnp
from jax import lax
from jax.experimental import pallas as pl
from jax.experimental.pallas import tpu as pltpu
from jax.sharding import PartitionSpec as P

LANES = 128
SUB = 8
highest = lax.Precision.HIGHEST
high = lax.Precision.HIGH


def inner_products(left, right, precision=high):
    return lax.dot_general(
        left, right, (((0,), (0,)), ((), ())), precision=precision, preferred_element_type=jnp.float32
    )


def matmul(left, right, precision=high):
    return jnp.dot(left, right, precision=precision, preferred_element_type=jnp.float32)


def split3(x):
    top = x.astype(jnp.bfloat16).astype(jnp.float32)
    rest = x - top
    mid = rest.astype(jnp.bfloat16).astype(jnp.float32)
    return top, mid, rest - mid


def rank_update(left, right):
    lt, lm, ll = split3(left)
    rt, rm, rl = split3(right)
    a = jnp.concatenate([lt, lt, lm, lt, ll, lm], axis=0).astype(jnp.bfloat16)
    b = jnp.concatenate([rt, rm, rt, rl, rt, rm], axis=0).astype(jnp.bfloat16)
    return lax.dot_general(a, b, (((0,), (0,)), ((), ())), preferred_element_type=jnp.float32)


def factor_diagonal(square, hook=None):
    lane = lax.broadcasted_iota(jnp.int32, (SUB, LANES), 1)
    sub = lax.broadcasted_iota(jnp.int32, (SUB, LANES), 0)
    full = (SUB, LANES)
    work = square
    upper_rows, inverse_rows = [], []
    for first in range(0, LANES, SUB):
        if hook is not None:
            hook(first // SUB)
        rows = work[:SUB]
        b = [jnp.broadcast_to(rows[t : t + 1, :], full) for t in range(SUB)]
        d = [
            [None if s < t else jnp.broadcast_to(b[t][:, first + s : first + s + 1], full) for s in range(SUB)]
            for t in range(SUB)
        ]
        inside = (lane >= first) & (lane < first + SUB)
        unit = [jnp.where(inside, jnp.where(lane == first + t, 1.0, 0.0), b[t]) for t in range(SUB)]
        tri = jnp.zeros(full, jnp.float32)
        out = jnp.zeros(full, jnp.float32)
        for t in range(SUB):
            inv = lax.rsqrt(d[t][t])
            inv = inv * (1.5 - 0.5 * (d[t][t] * inv) * inv)
            for s in range(t, SUB):
                d[t][s] = d[t][s] * inv
            x = unit[t] * inv
            for s in range(t + 1, SUB):
                for q in range(s, SUB):
                    d[s][q] = d[s][q] - d[t][s] * d[t][q]
                unit[s] = unit[s] - d[t][s] * x
            line = x
            for s in range(SUB):
                line = jnp.where(lane == first + s, d[t][s] if s >= t else 0.0, line)
            tri = jnp.where(sub == t, line, tri)
            out = jnp.where(sub == t, x, out)
        upper_rows.append(jnp.where(lane >= first, tri, 0.0))
        inverse_rows.append(jnp.where(lane < first + SUB, out, 0.0))
        if first + SUB < LANES:
            beyond = jnp.where(lane >= first + SUB, out, 0.0)
            left = work[SUB:]
            place = lax.broadcasted_iota(jnp.int32, left.shape, 1)
            left = jnp.where((place >= first) & (place < first + SUB), 0.0, left)
            work = left - rank_update(beyond, out)[first + SUB :]
    return jnp.concatenate(upper_rows, axis=0), jnp.concatenate(inverse_rows, axis=0)


def factor_kernel(gram_ref, upper_ref, inverse_ref, work):
    width = gram_ref.shape[0]
    work[...] = gram_ref[...]
    upper_ref[...] = jnp.zeros_like(upper_ref)
    inverse_ref[...] = jnp.zeros_like(inverse_ref)
    lanes_all = lax.broadcasted_iota(jnp.int32, (LANES, width), 1)

    @pl.loop(0, width // LANES)
    def _(k):
        at = pl.multiple_of(k * LANES, LANES)
        here = pl.ds(at, LANES)
        upper, inverse = factor_diagonal(work[here, here])
        rows = matmul(inverse, work[here, :], highest)
        upper_ref[here, :] = jnp.where(lanes_all >= at + LANES, rows, 0.0)
        upper_ref[here, here] = upper
        inverse_ref[here, :] = jnp.where(lanes_all < at, rows, 0.0)
        inverse_ref[here, here] = inverse
        work[here, :] = rows
        work[here, here] = inverse
        done = work[here, :]
        right = upper_ref[here, :]
        for i in range(1, width // LANES):
            @pl.when(i > k)
            def _():
                block = slice(i * LANES, (i + 1) * LANES)
                below = inner_products(right[:, block], done, highest)
                old = jnp.where((lanes_all >= at) & (lanes_all < at + LANES), 0.0, work[block, :])
                work[block, :] = old - below


def factor(gram):
    width = gram.shape[0]
    spec = pl.BlockSpec(memory_space=pltpu.VMEM)
    shape = jax.ShapeDtypeStruct((width, width), jnp.float32)
    return pl.pallas_call(
        factor_kernel,
        out_shape=(shape, shape),
        in_specs=[spec],
        out_specs=(spec, spec),
        scratch_shapes=[pltpu.VMEM((width, width), jnp.float32)],
        cost_estimate=pl.CostEstimate(
            flops=4 * width**3, bytes_accessed=12 * width * width, transcendentals=100000
        ),
        name="factor",
    )(gram)


def gram_kernel(nr, nc, part_ref, out_ref, heard, total, blocks, send, recv, give, take, pass_on, get):
    my_row = lax.axis_index("row")
    my_col = lax.axis_index("col")
    size = part_ref.shape[0] // nr
    wide = part_ref.shape[1]
    mesh_id = pl.DeviceIdType.MESH

    def rows_of(row):
        return pl.ds(pl.multiple_of(row * size, size), size)

    def row_peer(k):
        return lax.rem(my_row + k, nr)

    def col_peer(j):
        return lax.rem(my_col + j, nc)

    barrier = pltpu.get_barrier_semaphore()
    for k in range(1, nr):
        pl.semaphore_signal(barrier, inc=1, device_id=(row_peer(k), my_col), device_id_type=mesh_id)
    for j in range(1, nc):
        pl.semaphore_signal(barrier, inc=1, device_id=(my_row, col_peer(j)), device_id_type=mesh_id)
    pl.semaphore_wait(barrier, nr + nc - 2)

    first = [
        pltpu.make_async_remote_copy(
            src_ref=part_ref.at[rows_of(row_peer(k))],
            dst_ref=heard.at[k],
            send_sem=send.at[k],
            recv_sem=recv.at[k],
            device_id=(row_peer(k), my_col),
            device_id_type=mesh_id,
        )
        for k in range(1, nr)
    ]
    for copy in first:
        copy.start()
    value = part_ref[rows_of(my_row), :]
    for k, copy in enumerate(first, 1):
        copy.wait_recv()
        value = value + heard[k]
    total[...] = value

    def spread(k, j, block):
        return pltpu.make_async_remote_copy(
            src_ref=block,
            dst_ref=blocks.at[my_col, rows_of(lax.rem(my_row - k + nr, nr))],
            send_sem=pass_on.at[k, j],
            recv_sem=get.at[k, j],
            device_id=(my_row, col_peer(j)),
            device_id_type=mesh_id,
        )

    second = [
        pltpu.make_async_remote_copy(
            src_ref=total,
            dst_ref=blocks.at[my_col, rows_of(my_row)],
            send_sem=give.at[k],
            recv_sem=take.at[k],
            device_id=(row_peer(k), my_col),
            device_id_type=mesh_id,
        )
        for k in range(1, nr)
    ]
    for copy in second:
        copy.start()
    third = [spread(0, j, total) for j in range(1, nc)]
    for copy in third:
        copy.start()
    blocks[my_col, rows_of(my_row), :] = value
    for k, copy in enumerate(second, 1):
        copy.wait_recv()
        block = blocks.at[my_col, rows_of(lax.rem(my_row - k + nr, nr))]
        for j in range(1, nc):
            hop = spread(k, j, block)
            hop.start()
            third.append(hop)
    for copy in third:
        copy.wait_recv()
    for c in range(nc):
        out_ref[:, c * wide : (c + 1) * wide] = blocks[c]
    for copy in first + second + third:
        copy.wait_send()


def sum_gram(part, nr, nc):
    width, wide = part.shape
    spec = pl.BlockSpec(memory_space=pltpu.VMEM)
    dma = pltpu.SemaphoreType.DMA
    return pl.pallas_call(
        functools.partial(gram_kernel, nr, nc),
        out_shape=jax.ShapeDtypeStruct((width, wide * nc), jnp.float32),
        in_specs=[spec],
        out_specs=spec,
        scratch_shapes=[
            pltpu.VMEM((nr, width // nr, wide), jnp.float32),
            pltpu.VMEM((width // nr, wide), jnp.float32),
            pltpu.VMEM((nc, width, wide), jnp.float32),
            dma((nr,)),
            dma((nr,)),
            dma((nr,)),
            dma((nr,)),
            dma((nr, nc)),
            dma((nr, nc)),
        ],
        compiler_params=pltpu.CompilerParams(collective_id=0, has_side_effects=True),
        cost_estimate=pl.CostEstimate(
            flops=100000, bytes_accessed=20000000, transcendentals=0
        ),
        name="sum_gram",
    )(part)


def split2(x):
    top = x.astype(jnp.bfloat16)
    return top, (x - top.astype(jnp.float32)).astype(jnp.bfloat16)


def dot3(left, right, dims=(((1,), (0,)), ((), ()))):
    def one(a, b):
        return lax.dot_general(a, b, dims, preferred_element_type=jnp.float32)

    return one(left[0], right[0]) + (one(left[0], right[1]) + one(left[1], right[0]))


def update_kernel(panel_ref, weights_ref, trailing_ref, out_ref, top, low):
    @pl.when(pl.program_id(0) == 0)
    def _():
        top[...], low[...] = split2(weights_ref[...])

    pt, pm = split2(panel_ref[...])

    def product(left, right):
        return jnp.dot(left, right[...], preferred_element_type=jnp.float32)

    out_ref[...] = trailing_ref[...] - (product(pt, top) + (product(pt, low) + product(pm, top)))


def update(panel, weights, trailing):
    rows, width = panel.shape
    columns = trailing.shape[1]
    tile = next((t for t in (384, 256, 128, 64, 8) if rows % t == 0), rows)
    return pl.pallas_call(
        update_kernel,
        grid=(rows // tile,),
        out_shape=jax.ShapeDtypeStruct(trailing.shape, jnp.float32),
        in_specs=[
            pl.BlockSpec((tile, width), lambda i: (i, 0)),
            pl.BlockSpec((width, columns), lambda i: (0, 0)),
            pl.BlockSpec((tile, columns), lambda i: (i, 0)),
        ],
        out_specs=pl.BlockSpec((tile, columns), lambda i: (i, 0)),
        scratch_shapes=[pltpu.VMEM((width, columns), jnp.bfloat16)] * 2,
        cost_estimate=pl.CostEstimate(
            flops=6 * rows * width * columns,
            bytes_accessed=4 * (rows * width + 2 * rows * columns),
            transcendentals=0,
        ),
        name="update",
    )(panel, weights, trailing)


def gather_kernel(nc, pieces, block_ref, out_ref, send, recv, pass_on, get, near):
    my_row = lax.axis_index("row")
    my_col = lax.axis_index("col")
    rows, wide = block_ref.shape
    size = rows // pieces
    mesh_id = pl.DeviceIdType.MESH
    core = lax.rem(my_col, 2)
    partner = my_col + 1 - 2 * core

    def across(j):
        return lax.rem(my_col + 2 * j, nc)

    def columns(col):
        return pl.ds(pl.multiple_of(col * wide, wide), wide)

    def remote(src, dst, send_sem, recv_sem, col):
        return pltpu.make_async_remote_copy(
            src_ref=src, dst_ref=dst, send_sem=send_sem, recv_sem=recv_sem,
            device_id=(my_row, col), device_id_type=mesh_id,
        )

    barrier = pltpu.get_barrier_semaphore()
    pl.semaphore_signal(barrier, inc=1, device_id=(my_row, partner), device_id_type=mesh_id)
    for j in range(1, nc // 2):
        pl.semaphore_signal(barrier, inc=1, device_id=(my_row, across(j)), device_id_type=mesh_id)
    pl.semaphore_wait(barrier, nc // 2)

    far = []
    for p in range(pieces):
        here = pl.ds(p * size, size)
        for j in range(1, nc // 2):
            copy = remote(
                block_ref.at[here], out_ref.at[here, columns(my_col)],
                send.at[j, p], recv.at[j, p], across(j),
            )
            copy.start()
            far.append((p, j, copy))
    beside = remote(block_ref, out_ref.at[:, columns(my_col)], near.at[0], near.at[1], partner)
    beside.start()
    own = pltpu.make_async_copy(block_ref, out_ref.at[:, columns(my_col)], near.at[2])
    own.start()
    for p, j, copy in far:
        copy.wait_recv()
        source = lax.rem(my_col - 2 * j + nc, nc)
        spot = out_ref.at[pl.ds(p * size, size), columns(source)]
        hop = remote(spot, spot, pass_on.at[j, p], get.at[j, p], partner)
        hop.start()
        hops.append(hop)
    own.wait()
    beside.wait()
    for hop in hops:
        hop.wait()
    for _, _, copy in far:
        copy.wait_send()


def gather_panel(block, nc):
    rows, wide = block.shape
    pieces = 8
    if nc % 2 or wide % LANES or rows % (SUB * pieces):
        return lax.all_gather(block, "col", axis=1, tiled=True)
    dma = pltpu.SemaphoreType.DMA
    return pl.pallas_call(
        functools.partial(gather_kernel, nc, pieces),
        out_shape=jax.ShapeDtypeStruct((rows, wide * nc), jnp.float32),
        in_specs=[pl.BlockSpec(memory_space=pltpu.VMEM)],
        out_specs=pl.BlockSpec(memory_space=pl.ANY),
        scratch_shapes=[dma((nc // 2, pieces))] * 4 + [dma((3,))],
        compiler_params=pltpu.CompilerParams(collective_id=1, has_side_effects=True),
        name="gather_panel",
    )(block)


def general(nr, nc, panel_block, trailing):
    gathered = gather_panel(panel_block, nc)
    share = inner_products(gathered, trailing)
    projected = lax.psum(share, "row")
    gathered, share = lax.optimization_barrier((gathered, share))
    gram = sum_gram(inner_products(gathered, panel_block), nr, nc)
    upper, inverse = factor(gram)
    coupling = matmul(inverse, projected)
    weights = inner_products(inverse, coupling)
    updated = update(gathered, weights, trailing)
    return (upper, coupling, updated)


class Place:
    def __init__(self, nr):
        self.nr, self.nx = nr, 2
        self.nz = nr // 2
        self.row, self.col = lax.axis_index("row"), lax.axis_index("col")
        self.z, self.x = self.row // 2, lax.rem(self.row, 2)
        self.y, self.core = self.col // 2, lax.rem(self.col, 2)
        self.partner = (self.row, self.y * 2 + 1 - self.core)
        self.across = (self.row, (1 - self.y) * 2 + self.core)
        self.beside = (self.z * 2 + 1 - self.x, self.col)

    def level(self, j):
        return lax.rem(self.z + j, self.nz)

    def along(self, j):
        return (self.level(j) * 2 + self.x, self.col)

    def far(self, dy, dr):
        y = self.y + dy - 2 * dy * self.y
        return (lax.rem(self.row + dr, self.nr), y * 2 + self.core)


def remote(src, dst, send, recv, device):
    return pltpu.make_async_remote_copy(
        src_ref=src, dst_ref=dst, send_sem=send, recv_sem=recv,
        device_id=device, device_id_type=pl.DeviceIdType.MESH,
    )


def part(start, size, multiple=None):
    if isinstance(start, int):
        return pl.ds(start, size)
    return pl.ds(pl.multiple_of(start, multiple or size), size)


class RowSum:
    def __init__(self, at, share, from_x, from_z, out, sems):
        self.at, self.share, self.from_x, self.from_z, self.out = at, share, from_x, from_z, out
        self.send, self.recv = sems.at[0], sems.at[1]
        self.half = share.shape[0] // 2
        self.slice = self.half // at.nz
        self.sent = []

    def go(self, stage, j, ends):
        def make():
            src, dst, device = ends()
            return remote(src, dst, self.send.at[stage, j], self.recv.at[stage, j], device)

        make().start()
        self.sent.append(make)

    def landed(self, stage, j, dst):
        remote(dst, dst, self.send.at[stage, j], self.recv.at[stage, j], self.at.beside).wait_recv()

    def rows(self, x, z):
        return part(x * self.half + z * self.slice, self.slice)

    def over_x(self):
        self.go(0, 0, lambda: (
            self.share.at[part((1 - self.at.x) * self.half, self.half)], self.from_x, self.at.beside
        ))

    def over_z(self):
        self.landed(0, 0, self.from_x)
        mine = part(self.at.x * self.half, self.half)
        self.share[mine, :] = self.share[mine, :] + self.from_x[...]
        for j in range(1, self.at.nz):
            self.go(1, j, lambda j=j: (
                self.share.at[self.rows(self.at.x, self.at.level(j))], self.from_z.at[j], self.at.along(j)
            ))

    def give(self):
        here = self.rows(self.at.x, self.at.z)
        value = self.share[here, :]
        for j in range(1, self.at.nz):
            self.landed(1, j, self.from_z.at[j])
            value = value + self.from_z[j]
        self.out[here, :] = value

        def spot():
            return self.out.at[self.rows(self.at.x, self.at.z)]

        for j in range(1, self.at.nz):
            self.go(2, j, lambda j=j: (spot(), spot(), self.at.along(j)))
        self.go(3, 0, lambda: (spot(), spot(), self.at.beside))

    def back_x(self):
        for j in range(1, self.at.nz):
            def spot(j=j):
                return self.out.at[self.rows(self.at.x, self.at.level(self.at.nz - j))]

            self.landed(2, j, spot())
            self.go(3, j, lambda spot=spot: (spot(), spot(), self.at.beside))

    def finish(self):
        for j in range(self.at.nz):
            self.landed(3, j, self.out.at[self.rows(1 - self.at.x, self.at.level((self.at.nz - j) % self.at.nz))])

    def close(self):
        for make in self.sent:
            make().wait_send()


def panel_kernel(
    nr, pieces, chunk, block_ref, trailing_ref, high_ref, low_ref, tbuf, upper_ref, inverse_ref, summed_ref,
    blk, tth, ttl, gpart, cpart, heard_o, heard_c, own_g, cross_g,
    share_o, share_r, from_x_o, from_z_o, out_o, from_x_r, from_z_r, out_r,
    dia, du, di, half_g, half_u, half_i, row_r, cross_x,
    near, ysend, yrecv, fsend, frecv, o_sems, oa_sems, c_sems, ca_sems, g_sems, sum_sems, local,
):
    at = Place(nr)
    rows, wide = block_ref.shape
    half = rows // 2
    y, core, col = at.y, at.core, at.col
    pair = 2 * y
    away = 2 * (1 - y)
    size = half // pieces
    quarter = half // 4

    fetch = pltpu.make_async_copy(trailing_ref, tbuf, local.at[0])
    fetch.start()
    keep = pltpu.make_async_copy(block_ref, blk.at[col], local.at[1])
    keep.start()

    peers = [(dy, dr) for dy in range(2) for dr in range(nr) if dy or dr]
    barrier = pltpu.get_barrier_semaphore()
    for dy, dr in peers:
        pl.semaphore_signal(barrier, inc=1, device_id=at.far(dy, dr), device_id_type=pl.DeviceIdType.MESH)
    pl.semaphore_signal(barrier, inc=1, device_id=at.partner, device_id_type=pl.DeviceIdType.MESH)
    pl.semaphore_wait(barrier, len(peers) + 1)

    beside = remote(block_ref, blk.at[col], near.at[0], near.at[1], at.partner)
    first = [
        remote(
            block_ref.at[part((1 - y) * half + p * size, size)],
            blk.at[col, part((1 - y) * half + p * size, size)],
            ysend.at[p], yrecv.at[p], at.across,
        )
        for p in range(pieces)
    ]
    second = []
    for b in range(2):
        for p in range(2):
            i = pieces + 2 * b + p
            spot = blk.at[pair + b, part(y * half + core * 2 * quarter + p * quarter, quarter)]
            second.append(remote(spot, spot, ysend.at[i], yrecv.at[i], at.across))
    queue = first + second

    def follow(i):
        if i + 2 < len(queue):
            queue[i].wait_send()
            queue[i + 2].start()

    def arrived(i):
        if i < pieces:
            block, where = away + core, part(y * half + i * size, size)
        else:
            b, p = divmod(i - pieces, 2)
            block, where = away + b, part((1 - y) * half + core * 2 * quarter + p * quarter, quarter)
        spot = blk.at[block, where]
        remote(spot, spot, ysend.at[i], yrecv.at[i], at.across).wait_recv()
        remote(spot, spot, fsend.at[i], frecv.at[i], at.partner).start()

    def handed(i):
        if i < pieces:
            block, where = away + 1 - core, part(y * half + i * size, size)
        else:
            b, p = divmod(i - pieces, 2)
            block, where = away + b, part((1 - y) * half + (1 - core) * 2 * quarter + p * quarter, quarter)
        spot = blk.at[block, where]
        remote(spot, spot, fsend.at[i], frecv.at[i], at.partner).wait_recv()

    beside.start()
    queue[0].start()
    queue[1].start()
    keep.wait()

    beside.wait_recv()
    gpart[...] = jnp.zeros_like(gpart)

    @pl.loop(0, rows // chunk)
    def _(i):
        here = part(i * chunk, chunk)
        turned = split2(blk[col, here, :].T)
        right = split2(jnp.concatenate([blk[pair, here, :], blk[pair + 1, here, :]], axis=1))
        own = part(pair * wide, 2 * wide)
        high_ref[here, own], low_ref[here, own] = right
        gpart[...] += dot3(turned, right)

    gslice = wide // nr
    sent = [beside]
    made = []

    def go(ends):
        remote(*ends()).start()
        made.append(lambda: remote(*ends()))

    scatter = []
    for dr in range(1, nr):
        copy = remote(
            gpart.at[part(at.far(0, dr)[0] * gslice, gslice)], heard_o.at[dr],
            o_sems.at[0, dr], o_sems.at[1, dr], at.far(0, dr),
        )
        copy.start()
        scatter.append(copy)
        sent.append(copy)

    fetch.wait()
    share_o[...] = jnp.zeros_like(share_o)

    @pl.loop(0, rows // chunk)
    def _(i):
        here = part(i * chunk, chunk)
        high_part, low_part = split2(tbuf[here, :].T)
        tth[:, here], ttl[:, here] = high_part, low_part
        own = part(pair * wide, 2 * wide)
        share_o[...] += dot3((high_part, low_part), (high_ref[here, own], low_ref[here, own]))

    sums = [RowSum(at, share_o, from_x_o, from_z_o, out_o, sum_sems.at[0])]
    for b in range(2):
        sums.append(RowSum(at, share_r.at[b], from_x_r.at[b], from_z_r.at[b], out_r.at[b], sum_sems.at[1 + b]))

    def own_gram_sum():
        value = gpart[part(at.row * gslice, gslice), :]
        for dr, copy in enumerate(scatter, 1):
            copy.wait_recv()
            value = value + heard_o[dr]

        def spot():
            return own_g.at[col, part(at.row * gslice, gslice)]

        spot()[...] = value
        for dy, dr in peers:
            go(lambda dy=dy, dr=dr: (spot(), spot(), oa_sems.at[0, dy, dr], oa_sems.at[1, dy, dr], at.far(dy, dr)))

    def own_gram_forward():
        for dy in range(2):
            block = at.far(dy, 0)[1]
            whose = own_g.at[block]
            for dr in range(nr):
                if dy or dr:
                    spot = own_g.at[block, part(at.far(0, (nr - dr) % nr)[0] * gslice, gslice)]
                    remote(spot, spot, oa_sems.at[0, dy, dr], oa_sems.at[1, dy, dr], at.partner).wait_recv()
            copy = remote(whose, whose, g_sems.at[0, dy], g_sems.at[1, dy], at.partner)
            copy.start()
            sent.append(copy)

    def own_gram_done(dy):
        spot = own_g.at[at.far(dy, 0)[1] + 1 - 2 * core]
        remote(spot, spot, g_sems.at[0, dy], g_sems.at[1, dy], at.partner).wait_recv()

    cslice = wide // (2 * nr)

    def cross_rows(dy, dr, back=False):
        row = lax.rem(at.row + ((nr - dr) % nr if back else dr), nr)
        other = y + dy - 2 * dy * y
        return part((other * nr + row) * cslice, cslice)

    def cross_scatter():
        for dy, dr in peers:
            copy = remote(
                cpart.at[cross_rows(dy, dr)], heard_c.at[dy, dr],
                c_sems.at[0, dy, dr], c_sems.at[1, dy, dr], at.far(dy, dr),
            )
            copy.start()
            sent.append(copy)

    def cross_sum():
        value = cpart[cross_rows(0, 0), :]
        for dy, dr in peers:
            spot = heard_c.at[dy, dr]
            remote(spot, spot, c_sems.at[0, dy, dr], c_sems.at[1, dy, dr], at.partner).wait_recv()
            value = value + heard_c[dy, dr]

        def spot():
            return cross_g.at[core, cross_rows(0, 0)]

        spot()[...] = value
        for dy, dr in peers:
            go(lambda dy=dy, dr=dr: (spot(), spot(), ca_sems.at[0, dy, dr], ca_sems.at[1, dy, dr], at.far(dy, dr)))

    def cross_forward():
        for dy, dr in peers:
            spot = cross_g.at[core, cross_rows(dy, dr, back=True)]
            remote(spot, spot, ca_sems.at[0, dy, dr], ca_sems.at[1, dy, dr], at.partner).wait_recv()
        go(lambda: (cross_g.at[core], cross_g.at[core], g_sems.at[0, 2], g_sems.at[1, 2], at.partner))

    def cross_done():
        spot = cross_g.at[1 - core]
        remote(spot, spot, g_sems.at[0, 2], g_sems.at[1, 2], at.partner).wait_recv()

    def keep_split(here, block, count, value):
        high_ref[here, part(block * wide, count * wide, wide)] = value[0]
        low_ref[here, part(block * wide, count * wide, wide)] = value[1]

    def first_products(p):
        here = part(y * half + p * size, size)
        right = split2(jnp.concatenate([blk[away, here, :], blk[away + 1, here, :]], axis=1))
        keep_split(here, away, 2, right)
        value = dot3((tth[:, here], ttl[:, here]), right)
        turned = split2(blk[core, here, :].T)
        right = split2(jnp.concatenate([blk[2, here, :], blk[3, here, :]], axis=1))
        cross = dot3(turned, right)
        if p:
            for b in range(2):
                share_r[b] += value[:, b * wide : (b + 1) * wide]
            cpart[...] += cross
        else:
            for b in range(2):
                share_r[b] = value[:, b * wide : (b + 1) * wide]
            cpart[...] = cross

    def second_products(b, p):
        for k in range(2):
            here = part((1 - y) * half + k * 2 * quarter + p * quarter, quarter)
            right = split2(blk[away + b, here, :])
            keep_split(here, away + b, 1, right)
            share_r[b] += dot3((tth[:, here], ttl[:, here]), right)

    sums[0].over_x()
    own_gram_sum()
    for p in range(pieces):
        arrived(p)
        follow(p)
        if p == 1:
            sums[0].over_z()
        if p:
            handed(p - 1)
            first_products(p - 1)
    handed(pieces - 1)
    first_products(pieces - 1)
    cross_scatter()
    own_gram_forward()
    own_gram_done(0)
    own_gram_done(1)
    sums[0].give()

    def late(b, p):
        handed(pieces + 2 * b + p)
        second_products(b, p)

    def come(b, p):
        arrived(pieces + 2 * b + p)
        follow(pieces + 2 * b + p)

    events = {
        (0, 4): [cross_sum],
        (0, 10): [sums[0].back_x],
        (1, 0): [lambda: come(0, 0)],
        (1, 4): [lambda: late(0, 0), cross_forward],
        (1, 12): [lambda: come(0, 1)],
        (2, 2): [lambda: late(0, 1), sums[1].over_x],
        (2, 6): [lambda: come(1, 0)],
        (2, 8): [lambda: late(1, 0), sums[1].over_z],
        (2, 13): [sums[1].give],
        (3, 0): [lambda: come(1, 1)],
        (3, 2): [lambda: late(1, 1), sums[2].over_x, sums[1].back_x],
        (3, 7): [sums[2].over_z],
        (3, 12): [sums[2].give],
    }

    def whole(left, right):
        return jnp.dot(left, right, precision=highest, preferred_element_type=jnp.float32)

    lo, hi = slice(0, wide), slice(wide, 2 * wide)
    both = slice(0, 2 * wide)

    def load_half(h):
        half_g[lo, :] = own_g[2 * h]
        half_g[hi, :] = own_g[2 * h + 1]

    upper_ref[...] = jnp.zeros_like(upper_ref)
    inverse_ref[...] = jnp.zeros_like(inverse_ref)
    load_half(0)
    dia[...] = half_g[lo, lo]

    def even(h):
        half_u[lo, lo], half_i[lo, lo] = du[...], di[...]
        rest = whole(di[...], half_g[lo, hi])
        row_r[...] = rest
        half_u[lo, hi] = rest
        half_u[hi, lo] = jnp.zeros_like(rest)
        half_i[lo, hi] = jnp.zeros_like(rest)
        dia[...] = half_g[hi, hi] - inner_products(rest, rest, highest)

    def odd(h):
        half_u[hi, hi], half_i[hi, hi] = du[...], di[...]
        below = inner_products(row_r[...], half_i[lo, lo], highest)
        half_i[hi, lo] = -whole(di[...], below)
        place = slice(h * 2 * wide, (h + 1) * 2 * wide)
        upper_ref[place, place] = half_u[...]
        inverse_ref[place, place] = half_i[...]

    top, end = slice(0, 2 * wide), slice(2 * wide, 4 * wide)

    def after0():
        even(0)

    def after1():
        odd(0)
        cross_done()
        load_half(1)
        corner = jnp.concatenate([cross_g[0], cross_g[1]], axis=0)
        right = whole(half_i[...], corner)
        cross_x[...] = right
        upper_ref[top, end] = right
        half_g[...] = half_g[...] - inner_products(right, right, highest)
        dia[...] = half_g[lo, lo]

    def after2():
        even(1)

    def after3():
        odd(1)
        below = inner_products(cross_x[...], inverse_ref[top, top], highest)
        inverse_ref[end, top] = -whole(half_i[...], below)

    @pl.loop(0, 4)
    def _(k):
        def hook(step):
            for (when, where), steps in events.items():
                if where == step:
                    @pl.when(k == when)
                    def _():
                        for one in steps:
                            one()

        du[...], di[...] = factor_diagonal(dia[...], hook)
        for when, step in enumerate((after0, after1, after2, after3)):
            pl.when(k == when)(step)

    sums[2].back_x()
    for one in sums:
        one.finish()
    summed_ref[:, part(pair * wide, 2 * wide)] = out_o[...]
    for b in range(2):
        summed_ref[:, part((away + b) * wide, wide)] = out_r[b]
    for copy in sent + queue[-2:]:
        copy.wait_send()
    for make in made:
        make().wait_send()
    for i in range(len(queue)):
        spot = blk.at[0, pl.ds(0, size if i < pieces else quarter)]
        remote(spot, spot, fsend.at[i], frecv.at[i], at.partner).wait_send()
    for one in sums:
        one.close()


def panel_pieces(rows, wide, nr, nc):
    if nc != 4 or nr % 2 or nr < 4 or wide % LANES or wide % (2 * SUB * nr) or rows % 8:
        return 0
    half = rows // 2
    if half % (4 * LANES):
        return 0
    return next((p for p in (3, 2) if half % (p * LANES) == 0), 0)


def factor_panel(block, trailing, nr, pieces):
    rows, wide = block.shape
    columns = trailing.shape[1]
    chunk = rows // 2 // pieces
    hbm, vmem = pl.BlockSpec(memory_space=pl.ANY), pl.BlockSpec(memory_space=pltpu.VMEM)
    f32, dma = jnp.float32, pltpu.SemaphoreType.DMA

    def room(*shape, dtype=f32):
        return pltpu.VMEM(shape, dtype)

    width = 4 * wide
    nz = nr // 2
    square = jax.ShapeDtypeStruct((width, width), f32)
    return pl.pallas_call(
        functools.partial(panel_kernel, nr, pieces, chunk),
        out_shape=(
            jax.ShapeDtypeStruct((rows, width), jnp.bfloat16), jax.ShapeDtypeStruct((rows, width), jnp.bfloat16),
            jax.ShapeDtypeStruct((rows, columns), f32), square, square,
            jax.ShapeDtypeStruct((columns, width), f32),
        ),
        in_specs=[hbm, hbm],
        out_specs=(vmem,) * 6,
        scratch_shapes=[
            room(4, rows, wide),
            room(columns, rows, dtype=jnp.bfloat16), room(columns, rows, dtype=jnp.bfloat16),

            room(wide, 2 * wide), room(wide, 2 * wide),
            room(nr, wide // nr, 2 * wide), room(2, nr, wide // (2 * nr), 2 * wide),
            room(4, wide, 2 * wide), room(2, wide, 2 * wide),
            room(columns, 2 * wide), room(2, columns, wide),
            room(columns // 2, 2 * wide), room(nz, columns // nr, 2 * wide), room(columns, 2 * wide),
            room(2, columns // 2, wide), room(2, nz, columns // nr, wide), room(2, columns, wide),
            room(wide, wide), room(wide, wide), room(wide, wide),
            room(2 * wide, 2 * wide), room(2 * wide, 2 * wide), room(2 * wide, 2 * wide),
            room(wide, wide), room(2 * wide, 2 * wide),
            dma((2,)), dma((pieces + 4,)), dma((pieces + 4,)), dma((pieces + 4,)), dma((pieces + 4,)),
            dma((2, nr)), dma((2, 2, nr)), dma((2, 2, nr)), dma((2, 2, nr)), dma((2, 3)),
            dma((3, 2, 4, nz)), dma((2,)),
        ],
        compiler_params=pltpu.CompilerParams(
            collective_id=2, has_side_effects=True, vmem_limit_bytes=36 * 1024 * 1024
        ),
        name="factor_panel",
    )(block, trailing)


def finish_kernel(
    high_ref, low_ref, trailing_ref, inverse_ref, summed_ref, upper_ref,
    out_ref, coupling_ref, triangle_ref, top, low,
):
    @pl.when(pl.program_id(0) == 0)
    def _():
        inverse = split2(inverse_ref[...])
        coupling = dot3(inverse, split2(summed_ref[...]), (((1,), (1,)), ((), ())))
        coupling_ref[...] = coupling
        triangle_ref[...] = upper_ref[...]
        turned = split2(inverse_ref[...].T)
        top[...], low[...] = split2(dot3(turned, split2(coupling)))

    tile = out_ref.shape[0]
    here = part(pl.program_id(0) * tile, tile)
    out_ref[...] = trailing_ref[here, :] - dot3((high_ref[here, :], low_ref[here, :]), (top[...], low[...]))


def finish(panel_high, panel_low, trailing, upper, inverse, summed):
    rows, width = panel_high.shape
    columns = trailing.shape[1]
    tile = next((t for t in (384, 256, 128, 64, 16) if rows % t == 0), rows)
    whole = pl.BlockSpec(memory_space=pltpu.VMEM)
    still = lambda shape: pl.BlockSpec(shape, lambda i: (0, 0))
    f32 = jnp.float32
    return pl.pallas_call(
        finish_kernel,
        grid=(rows // tile,),
        out_shape=(
            jax.ShapeDtypeStruct(trailing.shape, f32), jax.ShapeDtypeStruct((width, columns), f32),
            jax.ShapeDtypeStruct((width, width), f32),
        ),
        in_specs=[whole] * 6,
        out_specs=(pl.BlockSpec((tile, columns), lambda i: (i, 0)), still((width, columns)), still((width, width))),
        scratch_shapes=[pltpu.VMEM((width, columns), jnp.bfloat16)] * 2,
        compiler_params=pltpu.CompilerParams(vmem_limit_bytes=32 * 1024 * 1024),
        name="finish",
    )(panel_high, panel_low, trailing, inverse, summed, upper)


def on_device(nr, nc, panel_block, trailing):
    rows, wide = panel_block.shape
    pieces = panel_pieces(rows, wide, nr, nc)
    if not pieces or trailing.shape[1] % (SUB * nr):
        return general(nr, nc, panel_block, trailing)
    panel_block = pltpu.with_memory_space_constraint(panel_block, pltpu.HBM)
    updated, coupling, triangle = finish(*factor_panel(panel_block, trailing, nr, pieces))
    return (triangle, coupling, updated)


def solution(mesh):
    placed = (P("row", "col"), P("row", "col"))
    return jax.shard_map(
        functools.partial(on_device, mesh.shape["row"], mesh.shape["col"]),
        mesh=mesh,
        in_specs=placed,
        out_specs=(P(), P(None, "col"), P("row", "col")),
        check_vma=False,
    )
```

```python
import functools

import jax
import jax.numpy as jnp
from jax import lax
from jax.experimental import pallas as pl
from jax.experimental.pallas import tpu as pltpu
from jax.sharding import PartitionSpec as P

LANES = 128
SUB = 8
highest = lax.Precision.HIGHEST
high = lax.Precision.HIGH


def inner_products(left, right, precision=high):
    return lax.dot_general(
        left, right, (((0,), (0,)), ((), ())), precision=precision, preferred_element_type=jnp.float32
    )


def matmul(left, right, precision=high):
    return jnp.dot(left, right, precision=precision, preferred_element_type=jnp.float32)


def split3(x):
    top = x.astype(jnp.bfloat16).astype(jnp.float32)
    rest = x - top
    mid = rest.astype(jnp.bfloat16).astype(jnp.float32)
    return top, mid, rest - mid


def rank_update(left, right):
    lt, lm, ll = split3(left)
    rt, rm, rl = split3(right)
    a = jnp.concatenate([lt, lt, lm, lt, ll, lm], axis=0).astype(jnp.bfloat16)
    b = jnp.concatenate([rt, rm, rt, rl, rt, rm], axis=0).astype(jnp.bfloat16)
    return lax.dot_general(a, b, (((0,), (0,)), ((), ())), preferred_element_type=jnp.float32)


def factor_diagonal(square, hook=None):
    lane = lax.broadcasted_iota(jnp.int32, (SUB, LANES), 1)
    sub = lax.broadcasted_iota(jnp.int32, (SUB, LANES), 0)
    full = (SUB, LANES)
    work = square
    upper_rows, inverse_rows = [], []
    for first in range(0, LANES, SUB):
        if hook is not None:
            hook(first // SUB)
        rows = work[:SUB]
        b = [jnp.broadcast_to(rows[t : t + 1, :], full) for t in range(SUB)]
        d = [
            [None if s < t else jnp.broadcast_to(b[t][:, first + s : first + s + 1], full) for s in range(SUB)]
            for t in range(SUB)
        ]
        inside = (lane >= first) & (lane < first + SUB)
        unit = [jnp.where(inside, jnp.where(lane == first + t, 1.0, 0.0), b[t]) for t in range(SUB)]
        tri = jnp.zeros(full, jnp.float32)
        out = jnp.zeros(full, jnp.float32)
        for t in range(SUB):
            inv = lax.rsqrt(d[t][t])
            inv = inv * (1.5 - 0.5 * (d[t][t] * inv) * inv)
            for s in range(t, SUB):
                d[t][s] = d[t][s] * inv
            x = unit[t] * inv
            for s in range(t + 1, SUB):
                for q in range(s, SUB):
                    d[s][q] = d[s][q] - d[t][s] * d[t][q]
                unit[s] = unit[s] - d[t][s] * x
            line = x
            for s in range(SUB):
                line = jnp.where(lane == first + s, d[t][s] if s >= t else 0.0, line)
            tri = jnp.where(sub == t, line, tri)
            out = jnp.where(sub == t, x, out)
        upper_rows.append(jnp.where(lane >= first, tri, 0.0))
        inverse_rows.append(jnp.where(lane < first + SUB, out, 0.0))
        if first + SUB < LANES:
            beyond = jnp.where(lane >= first + SUB, out, 0.0)
            left = work[SUB:]
            place = lax.broadcasted_iota(jnp.int32, left.shape, 1)
            left = jnp.where((place >= first) & (place < first + SUB), 0.0, left)
            work = left - rank_update(beyond, out)[first + SUB :]
    return jnp.concatenate(upper_rows, axis=0), jnp.concatenate(inverse_rows, axis=0)


def factor_kernel(gram_ref, upper_ref, inverse_ref, work):
    width = gram_ref.shape[0]
    work[...] = gram_ref[...]
    upper_ref[...] = jnp.zeros_like(upper_ref)
    inverse_ref[...] = jnp.zeros_like(inverse_ref)
    lanes_all = lax.broadcasted_iota(jnp.int32, (LANES, width), 1)

    @pl.loop(0, width // LANES)
    def _(k):
        at = pl.multiple_of(k * LANES, LANES)
        here = pl.ds(at, LANES)
        upper, inverse = factor_diagonal(work[here, here])
        rows = matmul(inverse, work[here, :], highest)
        upper_ref[here, :] = jnp.where(lanes_all >= at + LANES, rows, 0.0)
        upper_ref[here, here] = upper
        inverse_ref[here, :] = jnp.where(lanes_all < at, rows, 0.0)
        inverse_ref[here, here] = inverse
        work[here, :] = rows
        work[here, here] = inverse
        done = work[here, :]
        right = upper_ref[here, :]
        for i in range(1, width // LANES):
            @pl.when(i > k)
            def _():
                block = slice(i * LANES, (i + 1) * LANES)
                below = inner_products(right[:, block], done, highest)
                old = jnp.where((lanes_all >= at) & (lanes_all < at + LANES), 0.0, work[block, :])
                work[block, :] = old - below


def factor(gram):
    width = gram.shape[0]
    spec = pl.BlockSpec(memory_space=pltpu.VMEM)
    shape = jax.ShapeDtypeStruct((width, width), jnp.float32)
    return pl.pallas_call(
        factor_kernel,
        out_shape=(shape, shape),
        in_specs=[spec],
        out_specs=(spec, spec),
        scratch_shapes=[pltpu.VMEM((width, width), jnp.float32)],
        cost_estimate=pl.CostEstimate(
            flops=4 * width**3, bytes_accessed=12 * width * width, transcendentals=100000
        ),
        name="factor",
    )(gram)


def gram_kernel(nr, nc, part_ref, out_ref, heard, total, blocks, send, recv, give, take, pass_on, get):
    my_row = lax.axis_index("row")
    my_col = lax.axis_index("col")
    size = part_ref.shape[0] // nr
    wide = part_ref.shape[1]
    mesh_id = pl.DeviceIdType.MESH

    def rows_of(row):
        return pl.ds(pl.multiple_of(row * size, size), size)

    def row_peer(k):
        return lax.rem(my_row + k, nr)

    def col_peer(j):
        return lax.rem(my_col + j, nc)

    barrier = pltpu.get_barrier_semaphore()
    for k in range(1, nr):
        pl.semaphore_signal(barrier, inc=1, device_id=(row_peer(k), my_col), device_id_type=mesh_id)
    for j in range(1, nc):
        pl.semaphore_signal(barrier, inc=1, device_id=(my_row, col_peer(j)), device_id_type=mesh_id)
    pl.semaphore_wait(barrier, nr + nc - 2)

    first = [
        pltpu.make_async_remote_copy(
            src_ref=part_ref.at[rows_of(row_peer(k))],
            dst_ref=heard.at[k],
            send_sem=send.at[k],
            recv_sem=recv.at[k],
            device_id=(row_peer(k), my_col),
            device_id_type=mesh_id,
        )
        for k in range(1, nr)
    ]
    for copy in first:
        copy.start()
    value = part_ref[rows_of(my_row), :]
    for k, copy in enumerate(first, 1):
        copy.wait_recv()
        value = value + heard[k]
    total[...] = value

    def spread(k, j, block):
        return pltpu.make_async_remote_copy(
            src_ref=block,
            dst_ref=blocks.at[my_col, rows_of(lax.rem(my_row - k + nr, nr))],
            send_sem=pass_on.at[k, j],
            recv_sem=get.at[k, j],
            device_id=(my_row, col_peer(j)),
            device_id_type=mesh_id,
        )

    second = [
        pltpu.make_async_remote_copy(
            src_ref=total,
            dst_ref=blocks.at[my_col, rows_of(my_row)],
            send_sem=give.at[k],
            recv_sem=take.at[k],
            device_id=(row_peer(k), my_col),
            device_id_type=mesh_id,
        )
        for k in range(1, nr)
    ]
    for copy in second:
        copy.start()
    third = [spread(0, j, total) for j in range(1, nc)]
    for copy in third:
        copy.start()
    blocks[my_col, rows_of(my_row), :] = value
    for k, copy in enumerate(second, 1):
        copy.wait_recv()
        block = blocks.at[my_col, rows_of(lax.rem(my_row - k + nr, nr))]
        for j in range(1, nc):
            hop = spread(k, j, block)
            hop.start()
            third.append(hop)
    for copy in third:
        copy.wait_recv()
    for c in range(nc):
        out_ref[:, c * wide : (c + 1) * wide] = blocks[c]
    for copy in first + second + third:
        copy.wait_send()


def sum_gram(part, nr, nc):
    width, wide = part.shape
    spec = pl.BlockSpec(memory_space=pltpu.VMEM)
    dma = pltpu.SemaphoreType.DMA
    return pl.pallas_call(
        functools.partial(gram_kernel, nr, nc),
        out_shape=jax.ShapeDtypeStruct((width, wide * nc), jnp.float32),
        in_specs=[spec],
        out_specs=spec,
        scratch_shapes=[
            pltpu.VMEM((nr, width // nr, wide), jnp.float32),
            pltpu.VMEM((width // nr, wide), jnp.float32),
            pltpu.VMEM((nc, width, wide), jnp.float32),
            dma((nr,)),
            dma((nr,)),
            dma((nr,)),
            dma((nr,)),
            dma((nr, nc)),
            dma((nr, nc)),
        ],
        compiler_params=pltpu.CompilerParams(collective_id=0, has_side_effects=True),
        cost_estimate=pl.CostEstimate(
            flops=100000, bytes_accessed=20000000, transcendentals=0
        ),
        name="sum_gram",
    )(part)


def split2(x):
    top = x.astype(jnp.bfloat16)
    return top, (x - top.astype(jnp.float32)).astype(jnp.bfloat16)


def dot3(left, right, dims=(((1,), (0,)), ((), ()))):
    def one(a, b):
        return lax.dot_general(a, b, dims, preferred_element_type=jnp.float32)

    return one(left[0], right[0]) + (one(left[0], right[1]) + one(left[1], right[0]))


def update_kernel(panel_ref, weights_ref, trailing_ref, out_ref, top, low):
    @pl.when(pl.program_id(0) == 0)
    def _():
        top[...], low[...] = split2(weights_ref[...])

    pt, pm = split2(panel_ref[...])

    def product(left, right):
        return jnp.dot(left, right[...], preferred_element_type=jnp.float32)

    out_ref[...] = trailing_ref[...] - (product(pt, top) + (product(pt, low) + product(pm, top)))


def update(panel, weights, trailing):
    rows, width = panel.shape
    columns = trailing.shape[1]
    tile = next((t for t in (384, 256, 128, 64, 8) if rows % t == 0), rows)
    return pl.pallas_call(
        update_kernel,
        grid=(rows // tile,),
        out_shape=jax.ShapeDtypeStruct(trailing.shape, jnp.float32),
        in_specs=[
            pl.BlockSpec((tile, width), lambda i: (i, 0)),
            pl.BlockSpec((width, columns), lambda i: (0, 0)),
            pl.BlockSpec((tile, columns), lambda i: (i, 0)),
        ],
        out_specs=pl.BlockSpec((tile, columns), lambda i: (i, 0)),
        scratch_shapes=[pltpu.VMEM((width, columns), jnp.bfloat16)] * 2,
        cost_estimate=pl.CostEstimate(
            flops=6 * rows * width * columns,
            bytes_accessed=4 * (rows * width + 2 * rows * columns),
            transcendentals=0,
        ),
        name="update",
    )(panel, weights, trailing)


def gather_kernel(nc, pieces, block_ref, out_ref, send, recv, pass_on, get, near):
    my_row = lax.axis_index("row")
    my_col = lax.axis_index("col")
    rows, wide = block_ref.shape
    size = rows // pieces
    mesh_id = pl.DeviceIdType.MESH
    core = lax.rem(my_col, 2)
    partner = my_col + 1 - 2 * core

    def across(j):
        return lax.rem(my_col + 2 * j, nc)

    def columns(col):
        return pl.ds(pl.multiple_of(col * wide, wide), wide)

    def remote(src, dst, send_sem, recv_sem, col):
        return pltpu.make_async_remote_copy(
            src_ref=src, dst_ref=dst, send_sem=send_sem, recv_sem=recv_sem,
            device_id=(my_row, col), device_id_type=mesh_id,
        )

    barrier = pltpu.get_barrier_semaphore()
    pl.semaphore_signal(barrier, inc=1, device_id=(my_row, partner), device_id_type=mesh_id)
    for j in range(1, nc // 2):
        pl.semaphore_signal(barrier, inc=1, device_id=(my_row, across(j)), device_id_type=mesh_id)
    pl.semaphore_wait(barrier, nc // 2)

    far = []
    for p in range(pieces):
        here = pl.ds(p * size, size)
        for j in range(1, nc // 2):
            copy = remote(
                block_ref.at[here], out_ref.at[here, columns(my_col)],
                send.at[j, p], recv.at[j, p], across(j),
            )
            copy.start()
            far.append((p, j, copy))
    beside = remote(block_ref, out_ref.at[:, columns(my_col)], near.at[0], near.at[1], partner)
    beside.start()
    own = pltpu.make_async_copy(block_ref, out_ref.at[:, columns(my_col)], near.at[2])
    own.start()
    for p, j, copy in far:
        copy.wait_recv()
        source = lax.rem(my_col - 2 * j + nc, nc)
        spot = out_ref.at[pl.ds(p * size, size), columns(source)]
        hop = remote(spot, spot, pass_on.at[j, p], get.at[j, p], partner)
        hop.start()
        hops.append(hop)
    own.wait()
    beside.wait()
    for hop in hops:
        hop.wait()
    for _, _, copy in far:
        copy.wait_send()


def gather_panel(block, nc):
    rows, wide = block.shape
    pieces = 8
    if nc % 2 or wide % LANES or rows % (SUB * pieces):
        return lax.all_gather(block, "col", axis=1, tiled=True)
    dma = pltpu.SemaphoreType.DMA
    return pl.pallas_call(
        functools.partial(gather_kernel, nc, pieces),
        out_shape=jax.ShapeDtypeStruct((rows, wide * nc), jnp.float32),
        in_specs=[pl.BlockSpec(memory_space=pltpu.VMEM)],
        out_specs=pl.BlockSpec(memory_space=pl.ANY),
        scratch_shapes=[dma((nc // 2, pieces))] * 4 + [dma((3,))],
        compiler_params=pltpu.CompilerParams(collective_id=1, has_side_effects=True),
        name="gather_panel",
    )(block)


def general(nr, nc, panel_block, trailing):
    gathered = gather_panel(panel_block, nc)
    share = inner_products(gathered, trailing)
    projected = lax.psum(share, "row")
    gathered, share = lax.optimization_barrier((gathered, share))
    gram = sum_gram(inner_products(gathered, panel_block), nr, nc)
    upper, inverse = factor(gram)
    coupling = matmul(inverse, projected)
    weights = inner_products(inverse, coupling)
    updated = update(gathered, weights, trailing)
    return (upper, coupling, updated)


class Place:
    def __init__(self, nr):
        self.nr, self.nx = nr, 2
        self.nz = nr // 2
        self.row, self.col = lax.axis_index("row"), lax.axis_index("col")
        self.z, self.x = self.row // 2, lax.rem(self.row, 2)
        self.y, self.core = self.col // 2, lax.rem(self.col, 2)
        self.partner = (self.row, self.y * 2 + 1 - self.core)
        self.across = (self.row, (1 - self.y) * 2 + self.core)
        self.beside = (self.z * 2 + 1 - self.x, self.col)

    def level(self, j):
        return lax.rem(self.z + j, self.nz)

    def along(self, j):
        return (self.level(j) * 2 + self.x, self.col)

    def far(self, dy, dr):
        y = self.y + dy - 2 * dy * self.y
        return (lax.rem(self.row + dr, self.nr), y * 2 + self.core)


def remote(src, dst, send, recv, device):
    return pltpu.make_async_remote_copy(
        src_ref=src, dst_ref=dst, send_sem=send, recv_sem=recv,
        device_id=device, device_id_type=pl.DeviceIdType.MESH,
    )


def part(start, size, multiple=None):
    if isinstance(start, int):
        return pl.ds(start, size)
    return pl.ds(pl.multiple_of(start, multiple or size), size)


class RowSum:
    def __init__(self, at, share, from_x, from_z, out, sems):
        self.at, self.share, self.from_x, self.from_z, self.out = at, share, from_x, from_z, out
        self.send, self.recv = sems.at[0], sems.at[1]
        self.half = share.shape[0] // 2
        self.slice = self.half // at.nz
        self.sent = []

    def go(self, stage, j, ends):
        def make():
            src, dst, device = ends()
            return remote(src, dst, self.send.at[stage, j], self.recv.at[stage, j], device)

        make().start()
        self.sent.append(make)

    def landed(self, stage, j, dst):
        remote(dst, dst, self.send.at[stage, j], self.recv.at[stage, j], self.at.beside).wait_recv()

    def rows(self, x, z):
        return part(x * self.half + z * self.slice, self.slice)

    def over_x(self):
        self.go(0, 0, lambda: (
            self.share.at[part((1 - self.at.x) * self.half, self.half)], self.from_x, self.at.beside
        ))

    def over_z(self):
        self.landed(0, 0, self.from_x)
        mine = part(self.at.x * self.half, self.half)
        self.share[mine, :] = self.share[mine, :] + self.from_x[...]
        for j in range(1, self.at.nz):
            self.go(1, j, lambda j=j: (
                self.share.at[self.rows(self.at.x, self.at.level(j))], self.from_z.at[j], self.at.along(j)
            ))

    def give(self):
        here = self.rows(self.at.x, self.at.z)
        value = self.share[here, :]
        for j in range(1, self.at.nz):
            self.landed(1, j, self.from_z.at[j])
            value = value + self.from_z[j]
        self.out[here, :] = value

        def spot():
            return self.out.at[self.rows(self.at.x, self.at.z)]

        for j in range(1, self.at.nz):
            self.go(2, j, lambda j=j: (spot(), spot(), self.at.along(j)))
        self.go(3, 0, lambda: (spot(), spot(), self.at.beside))

    def back_x(self):
        for j in range(1, self.at.nz):
            def spot(j=j):
                return self.out.at[self.rows(self.at.x, self.at.level(self.at.nz - j))]

            self.landed(2, j, spot())
            self.go(3, j, lambda spot=spot: (spot(), spot(), self.at.beside))

    def finish(self):
        for j in range(self.at.nz):
            self.landed(3, j, self.out.at[self.rows(1 - self.at.x, self.at.level((self.at.nz - j) % self.at.nz))])

    def close(self):
        for make in self.sent:
            make().wait_send()


def panel_kernel(
    nr, pieces, chunk, block_ref, trailing_ref, high_ref, low_ref, tbuf, upper_ref, inverse_ref, summed_ref,
    blk, tth, ttl, gpart, cpart, heard_o, heard_c, own_g, cross_g,
    share, from_x, from_z, summed, share_d, from_x_d, from_z_d, summed_d,
    dia, du, di, half_g, half_u, half_i, row_r, cross_x,
    near, ysend, yrecv, fsend, frecv, o_sems, oa_sems, c_sems, ca_sems, g_sems, sum_sems, local,
):
    at = Place(nr)
    rows, wide = block_ref.shape
    half = rows // 2
    y, core, col = at.y, at.core, at.col
    pair = 2 * y
    away = 2 * (1 - y)
    size = half // pieces
    quarter = half // 4
    middle = trailing_ref.shape[1] // 2

    fetch = pltpu.make_async_copy(trailing_ref, tbuf, local.at[0])
    fetch.start()
    keep = pltpu.make_async_copy(block_ref, blk.at[col], local.at[1])
    keep.start()

    peers = [(dy, dr) for dy in range(2) for dr in range(nr) if dy or dr]
    barrier = pltpu.get_barrier_semaphore()
    for dy, dr in peers:
        pl.semaphore_signal(barrier, inc=1, device_id=at.far(dy, dr), device_id_type=pl.DeviceIdType.MESH)
    pl.semaphore_signal(barrier, inc=1, device_id=at.partner, device_id_type=pl.DeviceIdType.MESH)
    pl.semaphore_wait(barrier, len(peers) + 1)

    beside = remote(block_ref, blk.at[col], near.at[0], near.at[1], at.partner)
    first = [
        remote(
            block_ref.at[part((1 - y) * half + p * size, size)],
            blk.at[col, part((1 - y) * half + p * size, size)],
            ysend.at[p], yrecv.at[p], at.across,
        )
        for p in range(pieces)
    ]
    second = []
    for b in range(2):
        for p in range(2):
            i = pieces + 2 * b + p
            spot = blk.at[pair + b, part(y * half + core * 2 * quarter + p * quarter, quarter)]
            second.append(remote(spot, spot, ysend.at[i], yrecv.at[i], at.across))
    queue = first + second

    passed = []

    def launch(i, after=None):
        if after is not None:
            queue[after].wait_send()
            passed.append(after)
        queue[i].start()

    def arrived(i):
        if i < pieces:
            block, where = away + core, part(y * half + i * size, size)
        else:
            b, p = divmod(i - pieces, 2)
            block, where = away + b, part((1 - y) * half + core * 2 * quarter + p * quarter, quarter)
        spot = blk.at[block, where]
        remote(spot, spot, ysend.at[i], yrecv.at[i], at.across).wait_recv()
        remote(spot, spot, fsend.at[i], frecv.at[i], at.partner).start()

    def handed(i):
        if i < pieces:
            block, where = away + 1 - core, part(y * half + i * size, size)
        else:
            b, p = divmod(i - pieces, 2)
            block, where = away + b, part((1 - y) * half + (1 - core) * 2 * quarter + p * quarter, quarter)
        spot = blk.at[block, where]
        remote(spot, spot, fsend.at[i], frecv.at[i], at.partner).wait_recv()

    beside.start()
    launch(0)
    launch(1)
    keep.wait()

    beside.wait_recv()
    gpart[...] = jnp.zeros_like(gpart)

    @pl.loop(0, rows // chunk)
    def _(i):
        here = part(i * chunk, chunk)
        turned = split2(blk[col, here, :].T)
        right = split2(jnp.concatenate([blk[pair, here, :], blk[pair + 1, here, :]], axis=1))
        own = part(pair * wide, 2 * wide)
        high_ref[here, own], low_ref[here, own] = right
        gpart[...] += dot3(turned, right)

    gslice = wide // nr
    sent = [beside]
    made = []

    def go(ends):
        remote(*ends()).start()
        made.append(lambda: remote(*ends()))

    scatter = []
    for dr in range(1, nr):
        copy = remote(
            gpart.at[part(at.far(0, dr)[0] * gslice, gslice)], heard_o.at[dr],
            o_sems.at[0, dr], o_sems.at[1, dr], at.far(0, dr),
        )
        copy.start()
        scatter.append(copy)
        sent.append(copy)

    launch(2, 0)

    fetch.wait()
    share[0], share[1] = jnp.zeros_like(share[0]), jnp.zeros_like(share[1])

    def own_products(first_one, last_one):
        @pl.loop(first_one, last_one)
        def _(i):
            here = part(i * chunk, chunk)
            high_part, low_part = split2(tbuf[here, :].T)
            tth[:, here], ttl[:, here] = high_part, low_part
            own = part(pair * wide, 2 * wide)
            value = dot3((high_part, low_part), (high_ref[here, own], low_ref[here, own]))
            share[0] += value[:, :wide]
            share[1] += value[:, wide:]

    stretch = rows // chunk // 3
    own_products(0, stretch)
    launch(3, 1)
    own_products(stretch, 2 * stretch)
    if pieces > 4:
        launch(4, 2)
    own_products(2 * stretch, rows // chunk)

    sums = [
        RowSum(at, share.at[u], from_x.at[u], from_z.at[u], summed.at[u], sum_sems.at[u]) for u in range(3)
    ] + [
        RowSum(at, share_d.at[u], from_x_d.at[u], from_z_d.at[u], summed_d.at[u], sum_sems.at[3 + u]) for u in range(2)
    ]

    def own_gram_sum():
        value = gpart[part(at.row * gslice, gslice), :]
        for dr, copy in enumerate(scatter, 1):
            copy.wait_recv()
            value = value + heard_o[dr]

        def spot():
            return own_g.at[col, part(at.row * gslice, gslice)]

        spot()[...] = value
        for dy, dr in peers:
            go(lambda dy=dy, dr=dr: (spot(), spot(), oa_sems.at[0, dy, dr], oa_sems.at[1, dy, dr], at.far(dy, dr)))

    def own_gram_forward():
        for dy in range(2):
            block = at.far(dy, 0)[1]
            whose = own_g.at[block]
            for dr in range(nr):
                if dy or dr:
                    spot = own_g.at[block, part(at.far(0, (nr - dr) % nr)[0] * gslice, gslice)]
                    remote(spot, spot, oa_sems.at[0, dy, dr], oa_sems.at[1, dy, dr], at.partner).wait_recv()
            copy = remote(whose, whose, g_sems.at[0, dy], g_sems.at[1, dy], at.partner)
            copy.start()
            sent.append(copy)

    def own_gram_done(dy):
        spot = own_g.at[at.far(dy, 0)[1] + 1 - 2 * core]
        remote(spot, spot, g_sems.at[0, dy], g_sems.at[1, dy], at.partner).wait_recv()

    cslice = wide // (2 * nr)

    def cross_rows(dy, dr, back=False):
        row = lax.rem(at.row + ((nr - dr) % nr if back else dr), nr)
        other = y + dy - 2 * dy * y
        return part((other * nr + row) * cslice, cslice)

    def cross_scatter():
        for dy, dr in peers:
            copy = remote(
                cpart.at[cross_rows(dy, dr)], heard_c.at[dy, dr],
                c_sems.at[0, dy, dr], c_sems.at[1, dy, dr], at.far(dy, dr),
            )
            copy.start()
            sent.append(copy)

    def cross_sum():
        value = cpart[cross_rows(0, 0), :]
        for dy, dr in peers:
            spot = heard_c.at[dy, dr]
            remote(spot, spot, c_sems.at[0, dy, dr], c_sems.at[1, dy, dr], at.partner).wait_recv()
            value = value + heard_c[dy, dr]

        def spot():
            return cross_g.at[core, cross_rows(0, 0)]

        spot()[...] = value
        for dy, dr in peers:
            go(lambda dy=dy, dr=dr: (spot(), spot(), ca_sems.at[0, dy, dr], ca_sems.at[1, dy, dr], at.far(dy, dr)))

    def cross_forward():
        for dy, dr in peers:
            spot = cross_g.at[core, cross_rows(dy, dr, back=True)]
            remote(spot, spot, ca_sems.at[0, dy, dr], ca_sems.at[1, dy, dr], at.partner).wait_recv()
        go(lambda: (cross_g.at[core], cross_g.at[core], g_sems.at[0, 2], g_sems.at[1, 2], at.partner))

    def cross_done():
        spot = cross_g.at[1 - core]
        remote(spot, spot, g_sems.at[0, 2], g_sems.at[1, 2], at.partner).wait_recv()

    def keep_split(here, block, count, value):
        high_ref[here, part(block * wide, count * wide, wide)] = value[0]
        low_ref[here, part(block * wide, count * wide, wide)] = value[1]

    def first_products(p):
        here = part(y * half + p * size, size)
        right = split2(jnp.concatenate([blk[away, here, :], blk[away + 1, here, :]], axis=1))
        keep_split(here, away, 2, right)
        value = dot3((tth[:, here], ttl[:, here]), right)
        turned = split2(blk[core, here, :].T)
        right = split2(jnp.concatenate([blk[2, here, :], blk[3, here, :]], axis=1))
        cross = dot3(turned, right)
        parts = [(share.at[2], value[:, :wide])] + [
            (share_d.at[u], value[u * middle : (u + 1) * middle, wide:]) for u in range(2)
        ]
        for where, what in parts + [(cpart, cross)]:
            if p:
                where[...] += what
            else:
                where[...] = what

    def second_products(b, p):
        for k in range(2):
            here = part((1 - y) * half + k * 2 * quarter + p * quarter, quarter)
            right = split2(blk[away + b, here, :])
            keep_split(here, away + b, 1, right)
            value = dot3((tth[:, here], ttl[:, here]), right)
            if b == 0:
                share[2] += value
            else:
                for u in range(2):
                    share_d[u] += value[u * middle : (u + 1) * middle]

    own_gram_sum()
    for i in range(5 if pieces > 4 else 4, pieces):
        launch(i, i - 2)
    sums[0].over_x()
    sums[1].over_x()

    def first_piece(p):
        handed(p)
        first_products(p)

    for p in range(pieces):
        arrived(p)
        if p:
            first_piece(p - 1)
        if p == pieces - 3:
            sums[0].over_z()
        if p == pieces - 2:
            sums[1].over_z()
    first_piece(pieces - 1)
    cross_scatter()
    launch(pieces)
    own_gram_forward()
    own_gram_done(0)
    own_gram_done(1)
    sums[0].give()

    def late(b, p):
        handed(pieces + 2 * b + p)
        second_products(b, p)

    def come(b, p):
        arrived(pieces + 2 * b + p)

    def cross_spread():
        cross_sum()
        for i in range(1, 4):
            launch(pieces + i)

    events = {
        (0, 5): [sums[1].give],
        (0, 10): [cross_spread],
        (0, 14): [lambda: come(0, 0)],
        (1, 1): [lambda: late(0, 0), sums[0].back_x],
        (1, 5): [sums[1].back_x],
        (1, 11): [cross_forward],
        (1, 13): [lambda: come(0, 1)],
        (2, 0): [lambda: late(0, 1), sums[2].over_x],
        (2, 2): [lambda: come(1, 0)],
        (2, 4): [lambda: late(1, 0)],
        (2, 10): [sums[2].over_z],
        (2, 12): [lambda: come(1, 1)],
        (2, 14): [lambda: late(1, 1), sums[3].over_x, sums[4].over_x],
        (3, 5): [sums[2].give],
        (3, 6): [sums[3].over_z],
        (3, 8): [sums[4].over_z],
        (3, 12): [sums[2].back_x, sums[3].give],
        (3, 14): [sums[4].give],
    }

    def whole(left, right):
        return jnp.dot(left, right, precision=highest, preferred_element_type=jnp.float32)

    lo, hi = slice(0, wide), slice(wide, 2 * wide)
    both = slice(0, 2 * wide)

    def load_half(h):
        half_g[lo, :] = own_g[2 * h]
        half_g[hi, :] = own_g[2 * h + 1]

    upper_ref[...] = jnp.zeros_like(upper_ref)
    inverse_ref[...] = jnp.zeros_like(inverse_ref)
    load_half(0)
    dia[...] = half_g[lo, lo]

    def even(h):
        half_u[lo, lo], half_i[lo, lo] = du[...], di[...]
        rest = whole(di[...], half_g[lo, hi])
        row_r[...] = rest
        half_u[lo, hi] = rest
        half_u[hi, lo] = jnp.zeros_like(rest)
        half_i[lo, hi] = jnp.zeros_like(rest)
        dia[...] = half_g[hi, hi] - inner_products(rest, rest, highest)

    def odd(h):
        half_u[hi, hi], half_i[hi, hi] = du[...], di[...]
        below = inner_products(row_r[...], half_i[lo, lo], highest)
        half_i[hi, lo] = -whole(di[...], below)
        place = slice(h * 2 * wide, (h + 1) * 2 * wide)
        upper_ref[place, place] = half_u[...]
        inverse_ref[place, place] = half_i[...]

    top, end = slice(0, 2 * wide), slice(2 * wide, 4 * wide)

    def after0():
        even(0)

    def after1():
        odd(0)
        cross_done()
        load_half(1)
        corner = jnp.concatenate([cross_g[0], cross_g[1]], axis=0)
        right = whole(half_i[...], corner)
        cross_x[...] = right
        upper_ref[top, end] = right
        half_g[...] = half_g[...] - inner_products(right, right, highest)
        dia[...] = half_g[lo, lo]

    def after2():
        even(1)

    def after3():
        odd(1)
        below = inner_products(cross_x[...], inverse_ref[top, top], highest)
        inverse_ref[end, top] = -whole(half_i[...], below)

    @pl.loop(0, 4)
    def _(k):
        def hook(step):
            for (when, where), steps in events.items():
                if where == step:
                    @pl.when(k == when)
                    def _():
                        for one in steps:
                            one()

        du[...], di[...] = factor_diagonal(dia[...], hook)
        for when, step in enumerate((after0, after1, after2, after3)):
            pl.when(k == when)(step)

    sums[3].back_x()
    sums[4].back_x()
    for one in sums:
        one.finish()
    for u, block in enumerate((pair, pair + 1, away)):
        summed_ref[:, part(block * wide, wide)] = summed[u]
    for u in range(2):
        summed_ref[u * middle : (u + 1) * middle, part((away + 1) * wide, wide)] = summed_d[u]
    for copy in sent:
        copy.wait_send()
    for i, piece in enumerate(queue):
        if i not in passed:
            piece.wait_send()
    for make in made:
        make().wait_send()
    for i in range(len(queue)):
        spot = blk.at[0, pl.ds(0, size if i < pieces else quarter)]
        remote(spot, spot, fsend.at[i], frecv.at[i], at.partner).wait_send()
    for one in sums:
        one.close()


def panel_pieces(rows, wide, nr, nc):
    if nc != 4 or nr % 2 or nr < 4 or wide % LANES or wide % (2 * SUB * nr) or rows % 8:
        return 0
    half = rows // 2
    if half % (4 * LANES):
        return 0
    return next((p for p in (6, 4) if half % (p * LANES) == 0), 0)


def factor_panel(block, trailing, nr, pieces):
    rows, wide = block.shape
    columns = trailing.shape[1]
    chunk = next(c for c in (512, 384, 256, 128) if rows % (3 * c) == 0) if rows % (3 * LANES) == 0 else LANES
    hbm, vmem = pl.BlockSpec(memory_space=pl.ANY), pl.BlockSpec(memory_space=pltpu.VMEM)
    f32, dma = jnp.float32, pltpu.SemaphoreType.DMA

    def room(*shape, dtype=f32):
        return pltpu.VMEM(shape, dtype)

    width = 4 * wide
    nz = nr // 2
    square = jax.ShapeDtypeStruct((width, width), f32)
    return pl.pallas_call(
        functools.partial(panel_kernel, nr, pieces, chunk),
        out_shape=(
            jax.ShapeDtypeStruct((rows, width), jnp.bfloat16), jax.ShapeDtypeStruct((rows, width), jnp.bfloat16),
            jax.ShapeDtypeStruct((rows, columns), f32), square, square,
            jax.ShapeDtypeStruct((columns, width), f32),
        ),
        in_specs=[hbm, hbm],
        out_specs=(vmem,) * 6,
        scratch_shapes=[
            room(4, rows, wide),
            room(columns, rows, dtype=jnp.bfloat16), room(columns, rows, dtype=jnp.bfloat16),

            room(wide, 2 * wide), room(wide, 2 * wide),
            room(nr, wide // nr, 2 * wide), room(2, nr, wide // (2 * nr), 2 * wide),
            room(4, wide, 2 * wide), room(2, wide, 2 * wide),
            room(3, columns, wide), room(3, columns // 2, wide), room(3, nz, columns // nr, wide),
            room(3, columns, wide), room(2, columns // 2, wide), room(2, columns // 4, wide),
            room(2, nz, columns // nr // 2, wide), room(2, columns // 2, wide),
            room(wide, wide), room(wide, wide), room(wide, wide),
            room(2 * wide, 2 * wide), room(2 * wide, 2 * wide), room(2 * wide, 2 * wide),
            room(wide, wide), room(2 * wide, 2 * wide),
            dma((2,)), dma((pieces + 4,)), dma((pieces + 4,)), dma((pieces + 4,)), dma((pieces + 4,)),
            dma((2, nr)), dma((2, 2, nr)), dma((2, 2, nr)), dma((2, 2, nr)), dma((2, 3)),
            dma((5, 2, 4, nz)), dma((2,)),
        ],
        compiler_params=pltpu.CompilerParams(
            collective_id=2, has_side_effects=True, vmem_limit_bytes=36 * 1024 * 1024
        ),
        name="factor_panel",
    )(block, trailing)


def finish_kernel(
    high_ref, low_ref, trailing_ref, inverse_ref, summed_ref, upper_ref,
    out_ref, coupling_ref, triangle_ref, top, low,
):
    @pl.when(pl.program_id(0) == 0)
    def _():
        inverse = split2(inverse_ref[...])
        coupling = dot3(inverse, split2(summed_ref[...]), (((1,), (1,)), ((), ())))
        coupling_ref[...] = coupling
        triangle_ref[...] = upper_ref[...]
        turned = split2(inverse_ref[...].T)
        top[...], low[...] = split2(dot3(turned, split2(coupling)))

    tile = out_ref.shape[0]
    here = part(pl.program_id(0) * tile, tile)
    out_ref[...] = trailing_ref[here, :] - dot3((high_ref[here, :], low_ref[here, :]), (top[...], low[...]))


def finish(panel_high, panel_low, trailing, upper, inverse, summed):
    rows, width = panel_high.shape
    columns = trailing.shape[1]
    tile = next((t for t in (384, 256, 128, 64, 16) if rows % t == 0), rows)
    whole = pl.BlockSpec(memory_space=pltpu.VMEM)
    still = lambda shape: pl.BlockSpec(shape, lambda i: (0, 0))
    f32 = jnp.float32
    return pl.pallas_call(
        finish_kernel,
        grid=(rows // tile,),
        out_shape=(
            jax.ShapeDtypeStruct(trailing.shape, f32), jax.ShapeDtypeStruct((width, columns), f32),
            jax.ShapeDtypeStruct((width, width), f32),
        ),
        in_specs=[whole] * 6,
        out_specs=(pl.BlockSpec((tile, columns), lambda i: (i, 0)), still((width, columns)), still((width, width))),
        scratch_shapes=[pltpu.VMEM((width, columns), jnp.bfloat16)] * 2,
        compiler_params=pltpu.CompilerParams(vmem_limit_bytes=32 * 1024 * 1024),
        name="finish",
    )(panel_high, panel_low, trailing, inverse, summed, upper)


def on_device(nr, nc, panel_block, trailing):
    rows, wide = panel_block.shape
    pieces = panel_pieces(rows, wide, nr, nc)
    if not pieces or trailing.shape[1] % (2 * SUB * nr):
        return general(nr, nc, panel_block, trailing)
    panel_block = pltpu.with_memory_space_constraint(panel_block, pltpu.HBM)
    updated, coupling, triangle = finish(*factor_panel(panel_block, trailing, nr, pieces))
    return (triangle, coupling, updated)


def solution(mesh):
    placed = (P("row", "col"), P("row", "col"))
    return jax.shard_map(
        functools.partial(on_device, mesh.shape["row"], mesh.shape["col"]),
        mesh=mesh,
        in_specs=placed,
        out_specs=(P(), P(None, "col"), P("row", "col")),
        check_vma=False,
    )
```

```python
import functools

import jax
import jax.numpy as jnp
from jax import lax
from jax.experimental import pallas as pl
from jax.experimental.pallas import tpu as pltpu
from jax.sharding import PartitionSpec as P

LANES = 128
SUB = 8
highest = lax.Precision.HIGHEST
high = lax.Precision.HIGH


def inner_products(left, right, precision=high):
    return lax.dot_general(
        left, right, (((0,), (0,)), ((), ())), precision=precision, preferred_element_type=jnp.float32
    )


def matmul(left, right, precision=high):
    return jnp.dot(left, right, precision=precision, preferred_element_type=jnp.float32)


def split3(x):
    top = x.astype(jnp.bfloat16).astype(jnp.float32)
    rest = x - top
    mid = rest.astype(jnp.bfloat16).astype(jnp.float32)
    return top, mid, rest - mid


def rank_update(left, right):
    lt, lm, ll = split3(left)
    rt, rm, rl = split3(right)
    a = jnp.concatenate([lt, lt, lm, lt, ll, lm], axis=0).astype(jnp.bfloat16)
    b = jnp.concatenate([rt, rm, rt, rl, rt, rm], axis=0).astype(jnp.bfloat16)
    return lax.dot_general(a, b, (((0,), (0,)), ((), ())), preferred_element_type=jnp.float32)


def factor_diagonal(square, hook=None):
    lane = lax.broadcasted_iota(jnp.int32, (SUB, LANES), 1)
    sub = lax.broadcasted_iota(jnp.int32, (SUB, LANES), 0)
    full = (SUB, LANES)

    def row(value, t):
        return jnp.broadcast_to(value[t : t + 1, :], full)

    def column(value, t):
        return jnp.broadcast_to(value[:, t : t + 1], full)

    def corner(b, first):
        return [[None if s < t else column(b[t], first + s) for s in range(SUB)] for t in range(SUB)]

    work = square
    b = [row(work, t) for t in range(SUB)]
    d = corner(b, 0)
    upper_rows, inverse_rows = [], []
    for first in range(0, LANES, SUB):
        if hook is not None:
            hook(first // SUB)
        more = first + SUB < LANES
        if more:
            left = work[SUB:]
            place = lax.broadcasted_iota(jnp.int32, left.shape, 1)
            left = jnp.where((place >= first) & (place < first + SUB), 0.0, left)
            next_b = [row(left, t) for t in range(SUB)]
            next_d = corner(next_b, first + SUB)
        inside = (lane >= first) & (lane < first + SUB)
        unit = [jnp.where(inside, jnp.where(lane == first + t, 1.0, 0.0), b[t]) for t in range(SUB)]
        tri = jnp.zeros(full, jnp.float32)
        out = jnp.zeros(full, jnp.float32)
        for t in range(SUB):
            inv = lax.rsqrt(d[t][t])
            inv = inv * (1.5 - 0.5 * (d[t][t] * inv) * inv)
            for s in range(t, SUB):
                d[t][s] = d[t][s] * inv
            x = unit[t] * inv
            for s in range(t + 1, SUB):
                for q in range(s, SUB):
                    d[s][q] = d[s][q] - d[t][s] * d[t][q]
                unit[s] = unit[s] - d[t][s] * x
            line = x
            for s in range(SUB):
                line = jnp.where(lane == first + s, d[t][s] if s >= t else 0.0, line)
            tri = jnp.where(sub == t, line, tri)
            out = jnp.where(sub == t, x, out)
            if more:
                m = [column(x, first + SUB + s) for s in range(SUB)]
                for s in range(SUB):
                    next_b[s] = next_b[s] - m[s] * x
                    for q in range(s, SUB):
                        next_d[s][q] = next_d[s][q] - m[s] * m[q]
        upper_rows.append(jnp.where(lane >= first, tri, 0.0))
        inverse_rows.append(jnp.where(lane < first + SUB, out, 0.0))
        if more:
            beyond = jnp.where(lane >= first + SUB, out, 0.0)
            work = left - rank_update(beyond, out)[first + SUB :]
            b, d = next_b, next_d
    return jnp.concatenate(upper_rows, axis=0), jnp.concatenate(inverse_rows, axis=0)


def factor_kernel(gram_ref, upper_ref, inverse_ref, work):
    width = gram_ref.shape[0]
    work[...] = gram_ref[...]
    upper_ref[...] = jnp.zeros_like(upper_ref)
    inverse_ref[...] = jnp.zeros_like(inverse_ref)
    lanes_all = lax.broadcasted_iota(jnp.int32, (LANES, width), 1)

    @pl.loop(0, width // LANES)
    def _(k):
        at = pl.multiple_of(k * LANES, LANES)
        here = pl.ds(at, LANES)
        upper, inverse = factor_diagonal(work[here, here])
        rows = matmul(inverse, work[here, :], highest)
        upper_ref[here, :] = jnp.where(lanes_all >= at + LANES, rows, 0.0)
        upper_ref[here, here] = upper
        inverse_ref[here, :] = jnp.where(lanes_all < at, rows, 0.0)
        inverse_ref[here, here] = inverse
        work[here, :] = rows
        work[here, here] = inverse
        done = work[here, :]
        right = upper_ref[here, :]
        for i in range(1, width // LANES):
            @pl.when(i > k)
            def _():
                block = slice(i * LANES, (i + 1) * LANES)
                below = inner_products(right[:, block], done, highest)
                old = jnp.where((lanes_all >= at) & (lanes_all < at + LANES), 0.0, work[block, :])
                work[block, :] = old - below


def factor(gram):
    width = gram.shape[0]
    spec = pl.BlockSpec(memory_space=pltpu.VMEM)
    shape = jax.ShapeDtypeStruct((width, width), jnp.float32)
    return pl.pallas_call(
        factor_kernel,
        out_shape=(shape, shape),
        in_specs=[spec],
        out_specs=(spec, spec),
        scratch_shapes=[pltpu.VMEM((width, width), jnp.float32)],
        cost_estimate=pl.CostEstimate(
            flops=4 * width**3, bytes_accessed=12 * width * width, transcendentals=100000
        ),
        name="factor",
    )(gram)


def gram_kernel(nr, nc, part_ref, out_ref, heard, total, blocks, send, recv, give, take, pass_on, get):
    my_row = lax.axis_index("row")
    my_col = lax.axis_index("col")
    size = part_ref.shape[0] // nr
    wide = part_ref.shape[1]
    mesh_id = pl.DeviceIdType.MESH

    def rows_of(row):
        return pl.ds(pl.multiple_of(row * size, size), size)

    def row_peer(k):
        return lax.rem(my_row + k, nr)

    def col_peer(j):
        return lax.rem(my_col + j, nc)

    barrier = pltpu.get_barrier_semaphore()
    for k in range(1, nr):
        pl.semaphore_signal(barrier, inc=1, device_id=(row_peer(k), my_col), device_id_type=mesh_id)
    for j in range(1, nc):
        pl.semaphore_signal(barrier, inc=1, device_id=(my_row, col_peer(j)), device_id_type=mesh_id)
    pl.semaphore_wait(barrier, nr + nc - 2)

    first = [
        pltpu.make_async_remote_copy(
            src_ref=part_ref.at[rows_of(row_peer(k))],
            dst_ref=heard.at[k],
            send_sem=send.at[k],
            recv_sem=recv.at[k],
            device_id=(row_peer(k), my_col),
            device_id_type=mesh_id,
        )
        for k in range(1, nr)
    ]
    for copy in first:
        copy.start()
    value = part_ref[rows_of(my_row), :]
    for k, copy in enumerate(first, 1):
        copy.wait_recv()
        value = value + heard[k]
    total[...] = value

    def spread(k, j, block):
        return pltpu.make_async_remote_copy(
            src_ref=block,
            dst_ref=blocks.at[my_col, rows_of(lax.rem(my_row - k + nr, nr))],
            send_sem=pass_on.at[k, j],
            recv_sem=get.at[k, j],
            device_id=(my_row, col_peer(j)),
            device_id_type=mesh_id,
        )

    second = [
        pltpu.make_async_remote_copy(
            src_ref=total,
            dst_ref=blocks.at[my_col, rows_of(my_row)],
            send_sem=give.at[k],
            recv_sem=take.at[k],
            device_id=(row_peer(k), my_col),
            device_id_type=mesh_id,
        )
        for k in range(1, nr)
    ]
    for copy in second:
        copy.start()
    third = [spread(0, j, total) for j in range(1, nc)]
    for copy in third:
        copy.start()
    blocks[my_col, rows_of(my_row), :] = value
    for k, copy in enumerate(second, 1):
        copy.wait_recv()
        block = blocks.at[my_col, rows_of(lax.rem(my_row - k + nr, nr))]
        for j in range(1, nc):
            hop = spread(k, j, block)
            hop.start()
            third.append(hop)
    for copy in third:
        copy.wait_recv()
    for c in range(nc):
        out_ref[:, c * wide : (c + 1) * wide] = blocks[c]
    for copy in first + second + third:
        copy.wait_send()


def sum_gram(part, nr, nc):
    width, wide = part.shape
    spec = pl.BlockSpec(memory_space=pltpu.VMEM)
    dma = pltpu.SemaphoreType.DMA
    return pl.pallas_call(
        functools.partial(gram_kernel, nr, nc),
        out_shape=jax.ShapeDtypeStruct((width, wide * nc), jnp.float32),
        in_specs=[spec],
        out_specs=spec,
        scratch_shapes=[
            pltpu.VMEM((nr, width // nr, wide), jnp.float32),
            pltpu.VMEM((width // nr, wide), jnp.float32),
            pltpu.VMEM((nc, width, wide), jnp.float32),
            dma((nr,)),
            dma((nr,)),
            dma((nr,)),
            dma((nr,)),
            dma((nr, nc)),
            dma((nr, nc)),
        ],
        compiler_params=pltpu.CompilerParams(collective_id=0, has_side_effects=True),
        cost_estimate=pl.CostEstimate(
            flops=100000, bytes_accessed=20000000, transcendentals=0
        ),
        name="sum_gram",
    )(part)


def split2(x):
    top = x.astype(jnp.bfloat16)
    return top, (x - top.astype(jnp.float32)).astype(jnp.bfloat16)


def dot3(left, right, dims=(((1,), (0,)), ((), ()))):
    def one(a, b):
        return lax.dot_general(a, b, dims, preferred_element_type=jnp.float32)

    return one(left[0], right[0]) + (one(left[0], right[1]) + one(left[1], right[0]))


def update_kernel(panel_ref, weights_ref, trailing_ref, out_ref, top, low):
    @pl.when(pl.program_id(0) == 0)
    def _():
        top[...], low[...] = split2(weights_ref[...])

    pt, pm = split2(panel_ref[...])

    def product(left, right):
        return jnp.dot(left, right[...], preferred_element_type=jnp.float32)

    out_ref[...] = trailing_ref[...] - (product(pt, top) + (product(pt, low) + product(pm, top)))


def update(panel, weights, trailing):
    rows, width = panel.shape
    columns = trailing.shape[1]
    tile = next((t for t in (384, 256, 128, 64, 8) if rows % t == 0), rows)
    return pl.pallas_call(
        update_kernel,
        grid=(rows // tile,),
        out_shape=jax.ShapeDtypeStruct(trailing.shape, jnp.float32),
        in_specs=[
            pl.BlockSpec((tile, width), lambda i: (i, 0)),
            pl.BlockSpec((width, columns), lambda i: (0, 0)),
            pl.BlockSpec((tile, columns), lambda i: (i, 0)),
        ],
        out_specs=pl.BlockSpec((tile, columns), lambda i: (i, 0)),
        scratch_shapes=[pltpu.VMEM((width, columns), jnp.bfloat16)] * 2,
        cost_estimate=pl.CostEstimate(
            flops=6 * rows * width * columns,
            bytes_accessed=4 * (rows * width + 2 * rows * columns),
            transcendentals=0,
        ),
        name="update",
    )(panel, weights, trailing)


def gather_kernel(nc, pieces, block_ref, out_ref, send, recv, pass_on, get, near):
    my_row = lax.axis_index("row")
    my_col = lax.axis_index("col")
    rows, wide = block_ref.shape
    size = rows // pieces
    mesh_id = pl.DeviceIdType.MESH
    core = lax.rem(my_col, 2)
    partner = my_col + 1 - 2 * core

    def across(j):
        return lax.rem(my_col + 2 * j, nc)

    def columns(col):
        return pl.ds(pl.multiple_of(col * wide, wide), wide)

    def remote(src, dst, send_sem, recv_sem, col):
        return pltpu.make_async_remote_copy(
            src_ref=src, dst_ref=dst, send_sem=send_sem, recv_sem=recv_sem,
            device_id=(my_row, col), device_id_type=mesh_id,
        )

    barrier = pltpu.get_barrier_semaphore()
    pl.semaphore_signal(barrier, inc=1, device_id=(my_row, partner), device_id_type=mesh_id)
    for j in range(1, nc // 2):
        pl.semaphore_signal(barrier, inc=1, device_id=(my_row, across(j)), device_id_type=mesh_id)
    pl.semaphore_wait(barrier, nc // 2)

    far = []
    for p in range(pieces):
        here = pl.ds(p * size, size)
        for j in range(1, nc // 2):
            copy = remote(
                block_ref.at[here], out_ref.at[here, columns(my_col)],
                send.at[j, p], recv.at[j, p], across(j),
            )
            copy.start()
            far.append((p, j, copy))
    beside = remote(block_ref, out_ref.at[:, columns(my_col)], near.at[0], near.at[1], partner)
    beside.start()
    own = pltpu.make_async_copy(block_ref, out_ref.at[:, columns(my_col)], near.at[2])
    own.start()
    for p, j, copy in far:
        copy.wait_recv()
        source = lax.rem(my_col - 2 * j + nc, nc)
        spot = out_ref.at[pl.ds(p * size, size), columns(source)]
        hop = remote(spot, spot, pass_on.at[j, p], get.at[j, p], partner)
        hop.start()
        hops.append(hop)
    own.wait()
    beside.wait()
    for hop in hops:
        hop.wait()
    for _, _, copy in far:
        copy.wait_send()


def gather_panel(block, nc):
    rows, wide = block.shape
    pieces = 8
    if nc % 2 or wide % LANES or rows % (SUB * pieces):
        return lax.all_gather(block, "col", axis=1, tiled=True)
    dma = pltpu.SemaphoreType.DMA
    return pl.pallas_call(
        functools.partial(gather_kernel, nc, pieces),
        out_shape=jax.ShapeDtypeStruct((rows, wide * nc), jnp.float32),
        in_specs=[pl.BlockSpec(memory_space=pltpu.VMEM)],
        out_specs=pl.BlockSpec(memory_space=pl.ANY),
        scratch_shapes=[dma((nc // 2, pieces))] * 4 + [dma((3,))],
        compiler_params=pltpu.CompilerParams(collective_id=1, has_side_effects=True),
        name="gather_panel",
    )(block)


def general(nr, nc, panel_block, trailing):
    gathered = gather_panel(panel_block, nc)
    share = inner_products(gathered, trailing)
    projected = lax.psum(share, "row")
    gathered, share = lax.optimization_barrier((gathered, share))
    gram = sum_gram(inner_products(gathered, panel_block), nr, nc)
    upper, inverse = factor(gram)
    coupling = matmul(inverse, projected)
    weights = inner_products(inverse, coupling)
    updated = update(gathered, weights, trailing)
    return (upper, coupling, updated)


class Place:
    def __init__(self, nr):
        self.nr, self.nx = nr, 2
        self.nz = nr // 2
        self.row, self.col = lax.axis_index("row"), lax.axis_index("col")
        self.z, self.x = self.row // 2, lax.rem(self.row, 2)
        self.y, self.core = self.col // 2, lax.rem(self.col, 2)
        self.partner = (self.row, self.y * 2 + 1 - self.core)
        self.across = (self.row, (1 - self.y) * 2 + self.core)
        self.beside = (self.z * 2 + 1 - self.x, self.col)

    def level(self, j):
        return lax.rem(self.z + j, self.nz)

    def along(self, j):
        return (self.level(j) * 2 + self.x, self.col)

    def far(self, dy, dr):
        y = self.y + dy - 2 * dy * self.y
        return (lax.rem(self.row + dr, self.nr), y * 2 + self.core)


def remote(src, dst, send, recv, device):
    return pltpu.make_async_remote_copy(
        src_ref=src, dst_ref=dst, send_sem=send, recv_sem=recv,
        device_id=device, device_id_type=pl.DeviceIdType.MESH,
    )


def part(start, size, multiple=None):
    if isinstance(start, int):
        return pl.ds(start, size)
    return pl.ds(pl.multiple_of(start, multiple or size), size)


class RowSum:
    def __init__(self, at, share, from_x, from_z, out, sems):
        self.at, self.share, self.from_x, self.from_z, self.out = at, share, from_x, from_z, out
        self.send, self.recv = sems.at[0], sems.at[1]
        self.half = share.shape[0] // 2
        self.slice = self.half // at.nz
        self.sent = []

    def go(self, stage, j, ends):
        def make():
            src, dst, device = ends()
            return remote(src, dst, self.send.at[stage, j], self.recv.at[stage, j], device)

        make().start()
        self.sent.append(make)

    def landed(self, stage, j, dst):
        remote(dst, dst, self.send.at[stage, j], self.recv.at[stage, j], self.at.beside).wait_recv()

    def rows(self, x, z):
        return part(x * self.half + z * self.slice, self.slice)

    def over_x(self):
        self.go(0, 0, lambda: (
            self.share.at[part((1 - self.at.x) * self.half, self.half)], self.from_x, self.at.beside
        ))

    def over_z(self):
        self.landed(0, 0, self.from_x)
        mine = part(self.at.x * self.half, self.half)
        self.share[mine, :] = self.share[mine, :] + self.from_x[...]
        for j in range(1, self.at.nz):
            self.go(1, j, lambda j=j: (
                self.share.at[self.rows(self.at.x, self.at.level(j))], self.from_z.at[j], self.at.along(j)
            ))

    def give(self):
        here = self.rows(self.at.x, self.at.z)
        value = self.share[here, :]
        for j in range(1, self.at.nz):
            self.landed(1, j, self.from_z.at[j])
            value = value + self.from_z[j]
        self.out[here, :] = value

        def spot():
            return self.out.at[self.rows(self.at.x, self.at.z)]

        for j in range(1, self.at.nz):
            self.go(2, j, lambda j=j: (spot(), spot(), self.at.along(j)))
        self.go(3, 0, lambda: (spot(), spot(), self.at.beside))

    def back_x(self):
        for j in range(1, self.at.nz):
            def spot(j=j):
                return self.out.at[self.rows(self.at.x, self.at.level(self.at.nz - j))]

            self.landed(2, j, spot())
            self.go(3, j, lambda spot=spot: (spot(), spot(), self.at.beside))

    def finish(self):
        for j in range(self.at.nz):
            self.landed(3, j, self.out.at[self.rows(1 - self.at.x, self.at.level((self.at.nz - j) % self.at.nz))])

    def close(self):
        for make in self.sent:
            make().wait_send()


def panel_kernel(
    nr, pieces, chunk, block_ref, trailing_ref, high_ref, low_ref, tbuf, upper_ref, inverse_ref, summed_ref,
    blk, tth, ttl, gpart, cpart, heard_o, heard_c, own_g, cross_g,
    share, from_x, from_z, summed, share_d, from_x_d, from_z_d, summed_d,
    dia, du, di, half_g, half_u, half_i, row_r, cross_x,
    near, ysend, yrecv, fsend, frecv, o_sems, oa_sems, c_sems, ca_sems, g_sems, sum_sems, local,
):
    at = Place(nr)
    rows, wide = block_ref.shape
    half = rows // 2
    y, core, col = at.y, at.core, at.col
    pair = 2 * y
    away = 2 * (1 - y)
    size = half // pieces
    quarter = half // 4
    middle = trailing_ref.shape[1] // 2

    fetch = pltpu.make_async_copy(trailing_ref, tbuf, local.at[0])
    fetch.start()
    keep = pltpu.make_async_copy(block_ref, blk.at[col], local.at[1])
    keep.start()

    peers = [(dy, dr) for dy in range(2) for dr in range(nr) if dy or dr]
    barrier = pltpu.get_barrier_semaphore()
    for dy, dr in peers:
        pl.semaphore_signal(barrier, inc=1, device_id=at.far(dy, dr), device_id_type=pl.DeviceIdType.MESH)
    pl.semaphore_signal(barrier, inc=1, device_id=at.partner, device_id_type=pl.DeviceIdType.MESH)
    pl.semaphore_wait(barrier, len(peers) + 1)

    beside = remote(block_ref, blk.at[col], near.at[0], near.at[1], at.partner)
    first = [
        remote(
            block_ref.at[part((1 - y) * half + p * size, size)],
            blk.at[col, part((1 - y) * half + p * size, size)],
            ysend.at[p], yrecv.at[p], at.across,
        )
        for p in range(pieces)
    ]
    second = []
    for b in range(2):
        for p in range(2):
            i = pieces + 2 * b + p
            spot = blk.at[pair + b, part(y * half + core * 2 * quarter + p * quarter, quarter)]
            second.append(remote(spot, spot, ysend.at[i], yrecv.at[i], at.across))
    queue = first + second

    passed = []

    def launch(i, after=None):
        if after is not None:
            queue[after].wait_send()
            passed.append(after)
        queue[i].start()

    def arrived(i):
        if i < pieces:
            block, where = away + core, part(y * half + i * size, size)
        else:
            b, p = divmod(i - pieces, 2)
            block, where = away + b, part((1 - y) * half + core * 2 * quarter + p * quarter, quarter)
        spot = blk.at[block, where]
        remote(spot, spot, ysend.at[i], yrecv.at[i], at.across).wait_recv()
        remote(spot, spot, fsend.at[i], frecv.at[i], at.partner).start()

    def handed(i):
        if i < pieces:
            block, where = away + 1 - core, part(y * half + i * size, size)
        else:
            b, p = divmod(i - pieces, 2)
            block, where = away + b, part((1 - y) * half + (1 - core) * 2 * quarter + p * quarter, quarter)
        spot = blk.at[block, where]
        remote(spot, spot, fsend.at[i], frecv.at[i], at.partner).wait_recv()

    beside.start()
    launch(0)
    launch(1)
    keep.wait()

    beside.wait_recv()
    gpart[...] = jnp.zeros_like(gpart)

    @pl.loop(0, rows // chunk)
    def _(i):
        here = part(i * chunk, chunk)
        turned = split2(blk[col, here, :].T)
        right = split2(jnp.concatenate([blk[pair, here, :], blk[pair + 1, here, :]], axis=1))
        own = part(pair * wide, 2 * wide)
        high_ref[here, own], low_ref[here, own] = right
        gpart[...] += dot3(turned, right)

    gslice = wide // nr
    sent = [beside]
    made = []

    def go(ends):
        remote(*ends()).start()
        made.append(lambda: remote(*ends()))

    scatter = []
    for dr in range(1, nr):
        copy = remote(
            gpart.at[part(at.far(0, dr)[0] * gslice, gslice)], heard_o.at[dr],
            o_sems.at[0, dr], o_sems.at[1, dr], at.far(0, dr),
        )
        copy.start()
        scatter.append(copy)
        sent.append(copy)

    launch(2, 0)

    fetch.wait()
    share[0], share[1] = jnp.zeros_like(share[0]), jnp.zeros_like(share[1])

    def own_products(first_one, last_one):
        @pl.loop(first_one, last_one)
        def _(i):
            here = part(i * chunk, chunk)
            high_part, low_part = split2(tbuf[here, :].T)
            tth[:, here], ttl[:, here] = high_part, low_part
            own = part(pair * wide, 2 * wide)
            value = dot3((high_part, low_part), (high_ref[here, own], low_ref[here, own]))
            share[0] += value[:, :wide]
            share[1] += value[:, wide:]

    stretch = rows // chunk // 3
    own_products(0, stretch)
    launch(3, 1)
    own_products(stretch, 2 * stretch)
    if pieces > 4:
        launch(4, 2)
    own_products(2 * stretch, rows // chunk)

    sums = [
        RowSum(at, share.at[u], from_x.at[u], from_z.at[u], summed.at[u], sum_sems.at[u]) for u in range(3)
    ] + [
        RowSum(at, share_d.at[u], from_x_d.at[u], from_z_d.at[u], summed_d.at[u], sum_sems.at[3 + u]) for u in range(2)
    ]

    def own_gram_sum():
        value = gpart[part(at.row * gslice, gslice), :]
        for dr, copy in enumerate(scatter, 1):
            copy.wait_recv()
            value = value + heard_o[dr]

        def spot():
            return own_g.at[col, part(at.row * gslice, gslice)]

        spot()[...] = value
        for dy, dr in peers:
            go(lambda dy=dy, dr=dr: (spot(), spot(), oa_sems.at[0, dy, dr], oa_sems.at[1, dy, dr], at.far(dy, dr)))

    def own_gram_forward():
        for dy in range(2):
            block = at.far(dy, 0)[1]
            whose = own_g.at[block]
            for dr in range(nr):
                if dy or dr:
                    spot = own_g.at[block, part(at.far(0, (nr - dr) % nr)[0] * gslice, gslice)]
                    remote(spot, spot, oa_sems.at[0, dy, dr], oa_sems.at[1, dy, dr], at.partner).wait_recv()
            copy = remote(whose, whose, g_sems.at[0, dy], g_sems.at[1, dy], at.partner)
            copy.start()
            sent.append(copy)

    def own_gram_done(dy):
        spot = own_g.at[at.far(dy, 0)[1] + 1 - 2 * core]
        remote(spot, spot, g_sems.at[0, dy], g_sems.at[1, dy], at.partner).wait_recv()

    cslice = wide // (2 * nr)

    def cross_rows(dy, dr, back=False):
        row = lax.rem(at.row + ((nr - dr) % nr if back else dr), nr)
        other = y + dy - 2 * dy * y
        return part((other * nr + row) * cslice, cslice)

    def cross_scatter():
        for dy, dr in peers:
            copy = remote(
                cpart.at[cross_rows(dy, dr)], heard_c.at[dy, dr],
                c_sems.at[0, dy, dr], c_sems.at[1, dy, dr], at.far(dy, dr),
            )
            copy.start()
            sent.append(copy)

    def cross_sum():
        value = cpart[cross_rows(0, 0), :]
        for dy, dr in peers:
            spot = heard_c.at[dy, dr]
            remote(spot, spot, c_sems.at[0, dy, dr], c_sems.at[1, dy, dr], at.partner).wait_recv()
            value = value + heard_c[dy, dr]

        def spot():
            return cross_g.at[core, cross_rows(0, 0)]

        spot()[...] = value
        for dy, dr in peers:
            go(lambda dy=dy, dr=dr: (spot(), spot(), ca_sems.at[0, dy, dr], ca_sems.at[1, dy, dr], at.far(dy, dr)))

    def cross_forward():
        for dy, dr in peers:
            spot = cross_g.at[core, cross_rows(dy, dr, back=True)]
            remote(spot, spot, ca_sems.at[0, dy, dr], ca_sems.at[1, dy, dr], at.partner).wait_recv()
        go(lambda: (cross_g.at[core], cross_g.at[core], g_sems.at[0, 2], g_sems.at[1, 2], at.partner))

    def cross_done():
        spot = cross_g.at[1 - core]
        remote(spot, spot, g_sems.at[0, 2], g_sems.at[1, 2], at.partner).wait_recv()

    def keep_split(here, block, count, value):
        high_ref[here, part(block * wide, count * wide, wide)] = value[0]
        low_ref[here, part(block * wide, count * wide, wide)] = value[1]

    def first_products(p):
        here = part(y * half + p * size, size)
        right = split2(jnp.concatenate([blk[away, here, :], blk[away + 1, here, :]], axis=1))
        keep_split(here, away, 2, right)
        value = dot3((tth[:, here], ttl[:, here]), right)
        turned = split2(blk[core, here, :].T)
        right = split2(jnp.concatenate([blk[2, here, :], blk[3, here, :]], axis=1))
        cross = dot3(turned, right)
        parts = [(share.at[2], value[:, :wide])] + [
            (share_d.at[u], value[u * middle : (u + 1) * middle, wide:]) for u in range(2)
        ]
        for where, what in parts + [(cpart, cross)]:
            if p:
                where[...] += what
            else:
                where[...] = what

    def second_products(b, p):
        for k in range(2):
            here = part((1 - y) * half + k * 2 * quarter + p * quarter, quarter)
            right = split2(blk[away + b, here, :])
            keep_split(here, away + b, 1, right)
            value = dot3((tth[:, here], ttl[:, here]), right)
            if b == 0:
                share[2] += value
            else:
                for u in range(2):
                    share_d[u] += value[u * middle : (u + 1) * middle]

    own_gram_sum()
    for i in range(5 if pieces > 4 else 4, pieces):
        launch(i, i - 2)
    sums[0].over_x()
    sums[1].over_x()

    def first_piece(p):
        handed(p)
        first_products(p)

    for p in range(pieces):
        arrived(p)
        if p:
            first_piece(p - 1)
        if p == pieces - 3:
            sums[0].over_z()
        if p == pieces - 2:
            sums[1].over_z()
    first_piece(pieces - 1)
    cross_scatter()
    launch(pieces + 0)
    launch(pieces + 1)
    own_gram_forward()
    own_gram_done(0)
    own_gram_done(1)
    sums[0].give()

    def late(b, p):
        handed(pieces + 2 * b + p)
        second_products(b, p)

    def come(b, p):
        arrived(pieces + 2 * b + p)

    def cross_spread():
        cross_sum()
        for i in range(2, 4):
            launch(pieces + i)

    events = {
        (0, 5): [sums[1].give],
        (0, 10): [cross_spread],
        (0, 14): [lambda: come(0, 0)],
        (1, 1): [lambda: late(0, 0), sums[0].back_x],
        (1, 5): [sums[1].back_x],
        (1, 11): [cross_forward],
        (1, 13): [lambda: come(0, 1)],
        (2, 0): [lambda: late(0, 1), sums[2].over_x],
        (2, 2): [lambda: come(1, 0)],
        (2, 4): [lambda: late(1, 0)],
        (2, 10): [sums[2].over_z],
        (2, 12): [lambda: come(1, 1)],
        (2, 14): [lambda: late(1, 1), sums[3].over_x, sums[4].over_x],
        (3, 5): [sums[2].give],
        (3, 6): [sums[3].over_z],
        (3, 8): [sums[4].over_z],
        (3, 12): [sums[2].back_x, sums[3].give],
        (3, 14): [sums[4].give],
    }

    def whole(left, right):
        return jnp.dot(left, right, precision=highest, preferred_element_type=jnp.float32)

    lo, hi = slice(0, wide), slice(wide, 2 * wide)
    both = slice(0, 2 * wide)

    def load_half(h):
        half_g[lo, :] = own_g[2 * h]
        half_g[hi, :] = own_g[2 * h + 1]

    upper_ref[...] = jnp.zeros_like(upper_ref)
    inverse_ref[...] = jnp.zeros_like(inverse_ref)
    load_half(0)
    dia[...] = half_g[lo, lo]

    def even(h):
        half_u[lo, lo], half_i[lo, lo] = du[...], di[...]
        rest = whole(di[...], half_g[lo, hi])
        row_r[...] = rest
        half_u[lo, hi] = rest
        half_u[hi, lo] = jnp.zeros_like(rest)
        half_i[lo, hi] = jnp.zeros_like(rest)
        dia[...] = half_g[hi, hi] - inner_products(rest, rest, highest)

    def odd(h):
        half_u[hi, hi], half_i[hi, hi] = du[...], di[...]
        below = inner_products(row_r[...], half_i[lo, lo], highest)
        half_i[hi, lo] = -whole(di[...], below)
        place = slice(h * 2 * wide, (h + 1) * 2 * wide)
        upper_ref[place, place] = half_u[...]
        inverse_ref[place, place] = half_i[...]

    top, end = slice(0, 2 * wide), slice(2 * wide, 4 * wide)

    def after0():
        even(0)

    def after1():
        odd(0)
        cross_done()
        load_half(1)
        corner = jnp.concatenate([cross_g[0], cross_g[1]], axis=0)
        right = whole(half_i[...], corner)
        cross_x[...] = right
        upper_ref[top, end] = right
        half_g[...] = half_g[...] - inner_products(right, right, highest)
        dia[...] = half_g[lo, lo]

    def after2():
        even(1)

    def after3():
        odd(1)
        below = inner_products(cross_x[...], inverse_ref[top, top], highest)
        inverse_ref[end, top] = -whole(half_i[...], below)

    @pl.loop(0, 4)
    def _(k):
        def hook(step):
            for (when, where), steps in events.items():
                if where == step:
                    @pl.when(k == when)
                    def _():
                        for one in steps:
                            one()

        du[...], di[...] = factor_diagonal(dia[...], hook)
        for when, step in enumerate((after0, after1, after2, after3)):
            pl.when(k == when)(step)

    sums[3].back_x()
    sums[4].back_x()
    for one in sums:
        one.finish()
    for u, block in enumerate((pair, pair + 1, away)):
        summed_ref[:, part(block * wide, wide)] = summed[u]
    for u in range(2):
        summed_ref[u * middle : (u + 1) * middle, part((away + 1) * wide, wide)] = summed_d[u]
    for copy in sent:
        copy.wait_send()
    for i, piece in enumerate(queue):
        if i not in passed:
            piece.wait_send()
    for make in made:
        make().wait_send()
    for i in range(len(queue)):
        spot = blk.at[0, pl.ds(0, size if i < pieces else quarter)]
        remote(spot, spot, fsend.at[i], frecv.at[i], at.partner).wait_send()
    for one in sums:
        one.close()


def panel_pieces(rows, wide, nr, nc):
    if nc != 4 or nr % 2 or nr < 4 or wide % LANES or wide % (2 * SUB * nr) or rows % 8:
        return 0
    half = rows // 2
    if half % (4 * LANES):
        return 0
    return next((p for p in (6, 4) if half % (p * LANES) == 0), 0)


def factor_panel(block, trailing, nr, pieces):
    rows, wide = block.shape
    columns = trailing.shape[1]
    chunk = next(c for c in (512, 384, 256, 128) if rows % (3 * c) == 0) if rows % (3 * LANES) == 0 else LANES
    hbm, vmem = pl.BlockSpec(memory_space=pl.ANY), pl.BlockSpec(memory_space=pltpu.VMEM)
    f32, dma = jnp.float32, pltpu.SemaphoreType.DMA

    def room(*shape, dtype=f32):
        return pltpu.VMEM(shape, dtype)

    width = 4 * wide
    nz = nr // 2
    square = jax.ShapeDtypeStruct((width, width), f32)
    return pl.pallas_call(
        functools.partial(panel_kernel, nr, pieces, chunk),
        out_shape=(
            jax.ShapeDtypeStruct((rows, width), jnp.bfloat16), jax.ShapeDtypeStruct((rows, width), jnp.bfloat16),
            jax.ShapeDtypeStruct((rows, columns), f32), square, square,
            jax.ShapeDtypeStruct((columns, width), f32),
        ),
        in_specs=[hbm, hbm],
        out_specs=(vmem,) * 6,
        scratch_shapes=[
            room(4, rows, wide),
            room(columns, rows, dtype=jnp.bfloat16), room(columns, rows, dtype=jnp.bfloat16),

            room(wide, 2 * wide), room(wide, 2 * wide),
            room(nr, wide // nr, 2 * wide), room(2, nr, wide // (2 * nr), 2 * wide),
            room(4, wide, 2 * wide), room(2, wide, 2 * wide),
            room(3, columns, wide), room(3, columns // 2, wide), room(3, nz, columns // nr, wide),
            room(3, columns, wide), room(2, columns // 2, wide), room(2, columns // 4, wide),
            room(2, nz, columns // nr // 2, wide), room(2, columns // 2, wide),
            room(wide, wide), room(wide, wide), room(wide, wide),
            room(2 * wide, 2 * wide), room(2 * wide, 2 * wide), room(2 * wide, 2 * wide),
            room(wide, wide), room(2 * wide, 2 * wide),
            dma((2,)), dma((pieces + 4,)), dma((pieces + 4,)), dma((pieces + 4,)), dma((pieces + 4,)),
            dma((2, nr)), dma((2, 2, nr)), dma((2, 2, nr)), dma((2, 2, nr)), dma((2, 3)),
            dma((5, 2, 4, nz)), dma((2,)),
        ],
        compiler_params=pltpu.CompilerParams(
            collective_id=2, has_side_effects=True, vmem_limit_bytes=36 * 1024 * 1024
        ),
        name="factor_panel",
    )(block, trailing)


def finish_kernel(
    high_ref, low_ref, trailing_ref, inverse_ref, summed_ref, upper_ref,
    out_ref, coupling_ref, triangle_ref, top, low,
):
    @pl.when(pl.program_id(0) == 0)
    def _():
        inverse = split2(inverse_ref[...])
        coupling = dot3(inverse, split2(summed_ref[...]), (((1,), (1,)), ((), ())))
        coupling_ref[...] = coupling
        triangle_ref[...] = upper_ref[...]
        turned = split2(inverse_ref[...].T)
        top[...], low[...] = split2(dot3(turned, split2(coupling)))

    tile = out_ref.shape[0]
    here = part(pl.program_id(0) * tile, tile)
    out_ref[...] = trailing_ref[here, :] - dot3((high_ref[here, :], low_ref[here, :]), (top[...], low[...]))


def finish(panel_high, panel_low, trailing, upper, inverse, summed):
    rows, width = panel_high.shape
    columns = trailing.shape[1]
    tile = next((t for t in (384, 256, 128, 64, 16) if rows % t == 0), rows)
    whole = pl.BlockSpec(memory_space=pltpu.VMEM)
    still = lambda shape: pl.BlockSpec(shape, lambda i: (0, 0))
    f32 = jnp.float32
    return pl.pallas_call(
        finish_kernel,
        grid=(rows // tile,),
        out_shape=(
            jax.ShapeDtypeStruct(trailing.shape, f32), jax.ShapeDtypeStruct((width, columns), f32),
            jax.ShapeDtypeStruct((width, width), f32),
        ),
        in_specs=[whole] * 6,
        out_specs=(pl.BlockSpec((tile, columns), lambda i: (i, 0)), still((width, columns)), still((width, width))),
        scratch_shapes=[pltpu.VMEM((width, columns), jnp.bfloat16)] * 2,
        compiler_params=pltpu.CompilerParams(vmem_limit_bytes=32 * 1024 * 1024),
        name="finish",
    )(panel_high, panel_low, trailing, inverse, summed, upper)


def on_device(nr, nc, panel_block, trailing):
    rows, wide = panel_block.shape
    pieces = panel_pieces(rows, wide, nr, nc)
    if not pieces or trailing.shape[1] % (2 * SUB * nr):
        return general(nr, nc, panel_block, trailing)
    panel_block = pltpu.with_memory_space_constraint(panel_block, pltpu.HBM)
    updated, coupling, triangle = finish(*factor_panel(panel_block, trailing, nr, pieces))
    return (triangle, coupling, updated)


def solution(mesh):
    placed = (P("row", "col"), P("row", "col"))
    return jax.shard_map(
        functools.partial(on_device, mesh.shape["row"], mesh.shape["col"]),
        mesh=mesh,
        in_specs=placed,
        out_specs=(P(), P(None, "col"), P("row", "col")),
        check_vma=False,
    )
```
